512 devices in a mesh: member: 2 (over y), lon: 32 (over z), lat: 8 (over x, core).
Axes of the slice: x: 4, y: 2, z: 32, core: 2. Of those that a mesh axis runs over, the one named last changes fastest.
The devices are a block of a 4x8x32 slice.
Arguments:
- tracer: float32 [64, 128, 4096], P('member', 'lat', 'lon'), parts along dimension 0, may hold values from -6 to 6
- velocity: float32 [2, 64, 128, 4096], P(None, 'member', 'lat', 'lon'), parts along dimension 1, may hold values from -0.9 to 0.9
- surface: float32 [256, 4096], P(('member', 'lat'), 'lon'), parts along dimension 0, may hold values from -6 to 6
- transport: float32 [4, 128, 4096], P('member', 'lat', 'lon'), parts along dimension 0, may hold values from -3 to 3
- horiz_mixing: float32 [64], P('member'), parts along dimension 0, may hold values from 0.03 to 0.2
- vert_mixing: float32 [62], P('member'), parts along dimension 0, may hold values from 0.3 to 30
- levels: int32 [128, 4096], P('lat', 'lon'), may hold values from 0 to 32, as said below
- land_tiles: int32 [8, 32], P('lat', 'lon'), may hold values 0 or 1
- fold_pair: int32 [4096], P('lon'), may hold values from 0 to 4095, as said below
Outputs:
- tracer_new: float32 [64, 128, 4096], P('member', 'lat', 'lon'), parts along dimension 0
- surface_new: float32 [256, 4096], P(('member', 'lat'), 'lon'), parts along dimension 0
- transport_new: float32 [4, 128, 4096], P('member', 'lat', 'lon'), parts along dimension 0
The draws below stay inside these ranges and needn't reach their ends.
There are 2 independent parts, one for each index of `member`. The reference program is written for one: setup_inputs(seed, part) draws one part's arguments, and reference() takes and returns one part's arrays. A program takes and returns all parts, laid end to end along the dimension named above; an argument that names none is the same for every part. Nothing has to cross between parts.
Inputs may be any that keep to these rules, and one draw needn't show every extreme that they name: 0 marks a land cell, otherwise the count of sea levels. The fold pairing is a reflection: fold_pair[i] = (p - i) mod 4096 for one p in 0..4095, so fold_pair[fold_pair[i]] = i.
All inputs are finite; a program needn't handle non-finite values. No bound on the sum of `land_tiles` on one device may be relied on, other than what follows from the above.
Results may differ from the reference program's by a relative error of at most 0.00002.
Values sent between devices are 32-bit elements; how exact they have to be, the bound alone decides.
A program may use at most 64 MiB of HBM per device.

```python
import math
import jax
import jax.numpy as jnp

K = 32
SUB = 12
CLAT = 16
CLON = 128
NLAT = 128
NLON = 4096
N_LON = 32
N_LAT = 8


def draw_levels(key, part):
    land_key = jax.random.fold_in(key, 11)
    depth_key = jax.random.fold_in(key, 12)
    land_cells = jax.random.randint(land_key, (NLAT, NLON), 0, 5) == 0
    depth_draw = jax.random.randint(depth_key, (NLAT, NLON), 1, K + 1)
    return jnp.where(land_cells, 0, depth_draw).astype(jnp.int32)


def draw_fold_pair(key, part):
    pivot_key = jax.random.fold_in(key, 21)
    pivot_col = jax.random.randint(pivot_key, (), 0, NLON)
    return jnp.mod(pivot_col - jnp.arange(NLON, dtype=jnp.int32), NLON).astype(jnp.int32)


def set_ends(result, own_key, low, top_value):
    longest = result.shape.index(max(result.shape))
    spots = []
    for shift in (0, 1):
        where = [jax.random.randint(jax.random.fold_in(own_key, axis), (), 0, length) for axis, length in enumerate(result.shape)]
        where[longest] = (where[longest] + shift) % result.shape[longest]
        spots.append(tuple(where))
    return result.at[spots[0]].set(low).at[spots[1]].set(top_value)


def shard_levels(rng, shape, shards, least, top_value):
    loudness = 1.0
    for position, blocks in shards:
        draws = jax.random.uniform(jax.random.fold_in(jax.random.fold_in(rng, 6), position), (blocks,), jnp.float32, least / len(shards), top_value / len(shards))
        loudness = loudness * jnp.repeat(jnp.exp(draws), shape[position] // blocks).reshape((-1,) + (1,) * (len(shape) - 1 - position))
    return loudness


def noise(stream_key, dims, spread, reach, pieces=(), kind=jnp.bfloat16):
    result = spread * jax.random.normal(stream_key, dims, jnp.float32)
    if pieces:
        result = result * shard_levels(stream_key, dims, pieces, -0.22, 0.18)
    return jnp.clip(result, -reach, reach).astype(kind)


def setup_inputs(seed: int = 0, part: int = 0) -> dict:
    arg_keys = jax.random.split(jax.random.key(seed), 10)
    own_keys = jax.random.split(jax.random.fold_in(arg_keys[9], part), 10)
    return {
        "tracer": noise(own_keys[0], (K, NLAT, NLON), 1.0, 6.0, ((1, 8), (2, 32)), jnp.float32),
        "velocity": noise(own_keys[1], (2, K, NLAT, NLON), 0.15, 0.9, ((2, 8), (3, 32)), jnp.float32),
        "surface": noise(own_keys[2], (NLAT, NLON), 1.0, 6.0, ((0, 8), (1, 32)), jnp.float32),
        "transport": noise(own_keys[3], (2, NLAT, NLON), 0.5, 3.0, ((1, 8), (2, 32)), jnp.float32),
        "horiz_mixing": jnp.clip(jnp.exp(jax.random.uniform(own_keys[4], (K,), jnp.float32, math.log(0.03), math.log(0.2))), 0.03, 0.2),
        "vert_mixing": jnp.clip(jnp.exp(jax.random.uniform(own_keys[5], (K - 1,), jnp.float32, math.log(0.3), math.log(30.0))), 0.3, 30.0),
        "levels": draw_levels(jax.random.fold_in(arg_keys[9], 71), part),
        "land_tiles": set_ends((jax.random.randint(arg_keys[7], (N_LAT, N_LON), 0, 4) < 1).astype(jnp.int32), jax.random.fold_in(arg_keys[7], 1), 0, 1),
        "fold_pair": draw_fold_pair(jax.random.fold_in(arg_keys[9], 71), part),
    }


fb_step = 0.6
drag_rate = 0.02


def east_of(field):
    return jnp.roll(field, -1, axis=-1)


def west_of(field):
    return jnp.roll(field, 1, axis=-1)


def north_of(field, fold_pair):
    top_row = jnp.take(field[..., -1:, :], fold_pair, axis=-1)
    return jnp.concatenate([field[..., 1:, :], top_row], axis=-2)


def south_of(field):
    return jnp.concatenate([jnp.zeros_like(field[..., :1, :]), field[..., :-1, :]], axis=-2)


def face_flux(near_side, far_side, wet_near, wet_far, vel_near, vel_far, mixing):
    return wet_near * wet_far * (mixing * (far_side - near_side) - 0.25 * (vel_near + vel_far) * (near_side + far_side))


def thomas(stepped, coupling):
    depth_count = stepped.shape[0]
    primes = []
    sweeps = []
    for depth_idx in range(depth_count):
        diagonal_term = jnp.ones_like(stepped[depth_idx])
        if depth_idx > 0:
            diagonal_term = diagonal_term + coupling[depth_idx - 1]
        if depth_idx < depth_count - 1:
            diagonal_term = diagonal_term + coupling[depth_idx]
        if depth_idx > 0:
            pivot_term = diagonal_term + coupling[depth_idx - 1] * primes[depth_idx - 1]
            reduced = (stepped[depth_idx] + coupling[depth_idx - 1] * sweeps[depth_idx - 1]) / pivot_term
        else:
            pivot_term = diagonal_term
            reduced = stepped[depth_idx] / pivot_term
        if depth_idx < depth_count - 1:
            primes.append(-coupling[depth_idx] / pivot_term)
        else:
            primes.append(jnp.zeros_like(reduced))
        sweeps.append(reduced)
    solved = [None] * depth_count
    solved[depth_count - 1] = sweeps[depth_count - 1]
    for depth_idx in range(depth_count - 2, -1, -1):
        solved[depth_idx] = sweeps[depth_idx] - primes[depth_idx] * solved[depth_idx + 1]
    return jnp.stack(solved)


def reference(tracer, velocity, surface, transport, horiz_mixing, vert_mixing, levels, land_tiles, fold_pair):
    tile_land = jnp.repeat(jnp.repeat(land_tiles, CLAT, axis=0), CLON, axis=1)
    depth_levels = (levels * (1 - tile_land)).astype(jnp.int32)
    level_real = depth_levels.astype(jnp.float32)
    sea_cells = (depth_levels > 0).astype(jnp.float32)
    wet = (jnp.arange(K, dtype=jnp.int32)[:, None, None] < depth_levels[None]).astype(jnp.float32)

    mixing = horiz_mixing[:, None, None]
    zonal_vel = velocity[0]
    merid_vel = velocity[1]
    flux_east = face_flux(tracer, east_of(tracer), wet, east_of(wet), zonal_vel, east_of(zonal_vel), mixing)
    flux_north = face_flux(tracer, north_of(tracer, fold_pair), wet, north_of(wet, fold_pair), merid_vel, north_of(merid_vel, fold_pair), mixing)
    stepped = wet * (tracer + ((flux_east - west_of(flux_east)) + (flux_north - south_of(flux_north))))
    coupling = vert_mixing[:, None, None] * wet[1:]
    tracer_new = thomas(stepped, coupling)

    zonal_mask = sea_cells * east_of(sea_cells)
    zonal_depth = (level_real + east_of(level_real)) / (2.0 * K)
    merid_mask = sea_cells * north_of(sea_cells, fold_pair)
    merid_depth = (level_real + north_of(level_real, fold_pair)) / (2.0 * K)

    height = surface
    zonal = transport[0]
    merid = transport[1]
    for substep in range(SUB):
        divergence = (zonal - west_of(zonal)) + (merid - south_of(merid))
        height = (height - fb_step * divergence) * sea_cells
        east_vals = east_of(height)
        north_vals = north_of(height, fold_pair)
        zonal = (zonal * (1.0 - drag_rate) - fb_step * zonal_depth * (east_vals - height)) * zonal_mask
        merid = (merid * (1.0 - drag_rate) - fb_step * merid_depth * (north_vals - height)) * merid_mask
    return tracer_new, height, jnp.stack([zonal, merid])
```

```python
import functools

import jax
import jax.numpy as jnp
from jax import lax
from jax.experimental import pallas as pl
from jax.experimental.pallas import tpu as pltpu
from jax.sharding import PartitionSpec as P

SUB = 12
fb_step = 0.6
drag_rate = 0.02
MESH = pl.DeviceIdType.MESH

E, W, N, S, NE, NW, SE, SW = range(8)
OPPOSITE = {E: W, W: E, N: S, S: N, NE: SW, SW: NE, NW: SE, SE: NW}
STEP = {E: (0, 1), W: (0, -1), N: (1, 0), S: (-1, 0), NE: (1, 1), NW: (1, -1), SE: (-1, 1), SW: (-1, -1)}
REACH = (-3, -2, -1, 0, 1, 2, 3)
HOPS = (2, 4, 8)


def ocean_kernel(
    n_lon,
    n_lat,
    depth,
    rows,
    cols,
    tracer_hbm,
    velocity_hbm,
    surface_hbm,
    transport_hbm,
    levels_hbm,
    horiz,
    vert,
    land,
    fold,
    tracer_out,
    surface_out,
    transport_out,
    tr,
    vel,
    lev,
    own,
    halo,
    edge_lon,
    halo_lon,
    edge_lat,
    halo_lat,
    slab,
    hop_in,
    fin,
    tfin,
    step_ref,
    cpl,
    rec,
    prime,
    face_lat,
    mix_rows,
    ext,
    coef,
    fold_fix,
    load_sem,
    halo_send,
    halo_recv,
    trac_send,
    trac_recv,
    hop_send,
    hop_recv,
    fin_send,
    fin_recv,
    tfin_recv,
):
    lat = lax.axis_index("lat")
    lon = lax.axis_index("lon")
    top = lat == n_lat - 1
    bottom = lat == 0
    t_relay = n_lat - 3
    v_relay = 1
    is_t_relay = lat == t_relay
    is_v_relay = lat == v_relay
    relay = is_t_relay | is_v_relay

    def lon_at(step):
        return lax.rem(lon + step + n_lon, n_lon)

    def lat_at(step):
        return lax.rem(lat + step + n_lat, n_lat)

    def remote(src, dst, send, recv, to):
        return pltpu.make_async_remote_copy(
            src_ref=src, dst_ref=dst, send_sem=send, recv_sem=recv, device_id=to, device_id_type=MESH
        )

    small = [
        pltpu.make_async_copy(surface_hbm, own.at[pl.ds(0, rows)], load_sem.at[0]),
        pltpu.make_async_copy(transport_hbm, own.at[pl.ds(rows, 2 * rows)], load_sem.at[1]),
        pltpu.make_async_copy(levels_hbm, lev, load_sem.at[2]),
    ]
    large = [
        pltpu.make_async_copy(tracer_hbm, tr, load_sem.at[3]),
        pltpu.make_async_copy(velocity_hbm, vel, load_sem.at[4]),
    ]
    for copy in small:
        copy.start()
    barrier = pltpu.get_barrier_semaphore()
    peers = [STEP[side] for side in range(8)] + [(0, 2), (0, -2), (2, 0), (-2, 0)]
    for d_lat, d_lon in peers:
        pl.semaphore_signal(
            barrier, inc=1, device_id={"lat": lat_at(d_lat), "lon": lon_at(d_lon)}, device_id_type=MESH
        )
    for copy in large:
        copy.start()

    zeros_tile = jnp.zeros((4 * rows, cols), jnp.float32)

    @pl.when(bottom)
    def _():
        for side in (S, SE, SW):
            halo[side] = zeros_tile
        halo_lat[1] = jnp.zeros((2 * depth, cols), jnp.float32)

    @pl.when(top)
    def _():
        halo[N] = zeros_tile
        halo_lat[0] = jnp.zeros((2 * depth, cols), jnp.float32)

    for copy in small:
        copy.wait()
    dry = 1 - land[0, 0]
    own[pl.ds(3 * rows, rows), :] = (lev[...] * dry).astype(jnp.float32)

    @pl.when(top)
    def _():
        slab[0] = zeros_tile
        for i in range(12):
            last = rows - 1 - i
            slab[0, pl.ds(i, 1), :] = own[pl.ds(last, 1), :]
            slab[0, pl.ds(rows + i, 1), :] = -own[pl.ds(rows + last, 1), :]
            slab[0, pl.ds(2 * rows + i, 1), :] = own[pl.ds(3 * rows + last, 1), :]
            slab[0, pl.ds(3 * rows + i, 1), :] = -own[pl.ds(2 * rows + last - 1, 1), :]
        slab[0, pl.ds(3 * rows + 12, 1), :] = -own[pl.ds(3 * rows - 1, 1), :]

    pl.semaphore_wait(barrier, len(peers))

    def hop_copies(k, size):
        out = []
        for j, sign in enumerate((1, -1)):
            out.append(
                remote(
                    slab.at[k, pl.ds(0, size)],
                    hop_in.at[2 * k + j, pl.ds(0, size)],
                    hop_send.at[2 * k + j],
                    hop_recv.at[2 * k + j],
                    {"lon": lon_at(sign * HOPS[k])},
                )
            )
        return out

    pivot_col = lax.rem(fold[0] + lon * cols, n_lon * cols)
    q = pivot_col // cols
    r = pivot_col - q * cols
    q_odd = q - 1 + (q & 1)

    def turn(m):
        return ((q_odd - 2 * m + 15 + 4 * n_lon) & (n_lon - 1)) >> 1

    tau = turn(lon)

    def hop_start(k, size):
        for copy in hop_copies(k, size):
            copy.start()

    def hop_next(k, size):
        for copy in hop_copies(k, size):
            copy.wait_recv()
        bit = jnp.full((size, cols), (tau >> (k + 1)) & 1, jnp.int32)
        slab[k + 1, pl.ds(0, size), :] = jnp.where(
            bit == 0, hop_in[2 * k, pl.ds(0, size), :], hop_in[2 * k + 1, pl.ds(0, size), :]
        )

    @pl.when(top)
    def _():
        hop_start(0, 4 * rows)

    def halo_copy(side):
        d_lat, d_lon = STEP[side]
        slot = OPPOSITE[side]
        return remote(
            own,
            halo.at[slot],
            halo_send.at[side],
            halo_recv.at[slot],
            {"lat": lat_at(d_lat), "lon": lon_at(d_lon)},
        )

    def halo_wait(side):
        remote(own, halo.at[side], halo_send.at[side], halo_recv.at[side], {"lon": lon}).wait_recv()

    for side in (E, W):
        halo_copy(side).start()

    @pl.when(jnp.logical_not(top))
    def _():
        for side in (N, NE, NW):
            halo_copy(side).start()

    @pl.when(jnp.logical_not(bottom))
    def _():
        for side in (S, SE, SW):
            halo_copy(side).start()

    for copy in large:
        copy.wait()
    u_base = 0
    v_base = depth * rows
    edge_lat[0, pl.ds(0, depth), :] = tr[pl.ds(rows - 1, depth, stride=rows), :]
    edge_lat[0, pl.ds(depth, depth), :] = vel[pl.ds(v_base + rows - 1, depth, stride=rows), :]
    edge_lat[1, pl.ds(0, depth), :] = tr[pl.ds(0, depth, stride=rows), :]
    edge_lat[1, pl.ds(depth, depth), :] = vel[pl.ds(v_base, depth, stride=rows), :]

    def spread_copy(j):
        to = (t_relay, v_relay)[j]
        return remote(
            edge_lat.at[0, pl.ds(j * depth, depth)],
            slab.at[0, pl.ds(0, depth)],
            trac_send.at[j],
            trac_recv.at[4],
            {"lat": to},
        )

    def lat_copy(north):
        slot = 1 if north else 0
        return remote(
            edge_lat.at[0 if north else 1],
            halo_lat.at[slot],
            trac_send.at[0 if north else 2],
            trac_recv.at[slot],
            {"lat": lat_at(1 if north else -1)},
        )

    @pl.when(top)
    def _():
        spread_copy(0).start()
        spread_copy(1).start()

    @pl.when(jnp.logical_not(top))
    def _():
        lat_copy(True).start()

    @pl.when(jnp.logical_not(bottom))
    def _():
        lat_copy(False).start()

    lane8 = lax.broadcasted_iota(jnp.int32, (8, cols), 1)
    half = lane8 >> 1

    def pack(l, carry):
        pt, pu = carry
        for g in range(2):
            item = l + depth * g
            here = half == jnp.full((8, cols), item, jnp.int32)
            at = pl.multiple_of(l * rows + 8 * g, 8)
            pt = jnp.where(here, pltpu.roll(tr[pl.ds(at, 8), :], 2 * item + 1, axis=1), pt)
            pu = jnp.where(here, pltpu.roll(vel[pl.ds(at, 8), :], 2 * item + 1, axis=1), pu)
        return pt, pu

    pt, pu = lax.fori_loop(
        0, depth, pack, (jnp.zeros((8, cols), jnp.float32), jnp.zeros((8, cols), jnp.float32)), unroll=4
    )
    edge_lon[pl.ds(0, 8), :] = pt
    edge_lon[pl.ds(8, 8), :] = pu

    def lon_copy(east):
        slot = 1 if east else 0
        return remote(
            edge_lon,
            halo_lon.at[slot],
            trac_send.at[3 if east else 4],
            trac_recv.at[2 + slot],
            {"lon": lon_at(1 if east else -1)},
        )

    lon_copy(True).start()
    lon_copy(False).start()

    def trac_wait(dst, sem):
        remote(dst, dst, trac_send.at[5], sem, {"lon": lon}).wait_recv()

    @pl.when(relay)
    def _():
        trac_wait(slab.at[0, pl.ds(0, depth)], trac_recv.at[4])
        hop_start(0, depth)

    h_own = own[pl.ds(3 * rows, rows), :]

    def pivots(l, carry):
        c_up, p_up = carry
        wet_below = (jnp.full((rows, cols), (l + 1).astype(jnp.float32)) < h_own).astype(jnp.float32)
        c_down = vert[jnp.minimum(l, depth - 2)] * wet_below
        pivot = (1.0 + c_up + c_down) + c_up * p_up
        inv = 1.0 / pivot
        p_down = -c_down * inv
        at = pl.ds(pl.multiple_of(l * rows, rows), rows)
        cpl[at, :] = c_up
        rec[at, :] = inv
        prime[at, :] = p_down
        mix_rows[pl.ds(l, 1), :] = jnp.full((1, cols), horiz[l])
        return c_down, p_down

    zero = jnp.zeros((rows, cols), jnp.float32)
    lax.fori_loop(0, depth, pivots, (zero, zero), unroll=2)

    @pl.when(top)
    def _():
        hop_next(0, 4 * rows)
        hop_start(1, 4 * rows)

    @pl.when(relay)
    def _():
        hop_next(0, depth)
        hop_start(1, depth)

    for side in (E, W):
        halo_wait(side)

    @pl.when(jnp.logical_not(top))
    def _():
        for side in (N, NE, NW):
            halo_wait(side)

    @pl.when(jnp.logical_not(bottom))
    def _():
        for side in (S, SE, SW):
            halo_wait(side)

    lane16 = lax.broadcasted_iota(jnp.int32, (rows, cols), 1)
    row16 = lax.broadcasted_iota(jnp.int32, (rows, cols), 0)
    near = lane16 < cols // 2
    left, right = pl.ds(0, cols), pl.ds(cols, cols)
    for f in range(4):
        part = pl.ds(f * rows, rows)
        ext[f, pl.ds(0, rows), left] = halo[S, part, :]
        ext[f, pl.ds(0, rows), right] = jnp.where(near, halo[SE, part, :], halo[SW, part, :])
        ext[f, pl.ds(rows, rows), left] = own[part, :]
        ext[f, pl.ds(rows, rows), right] = jnp.where(near, halo[E, part, :], halo[W, part, :])

    fold_fix[...] = jnp.zeros((8, 2 * cols), jnp.float32)

    @pl.when(jnp.logical_not(top))
    def _():
        for f in range(4):
            part = pl.ds(f * rows, rows)
            ext[f, pl.ds(2 * rows, rows), left] = halo[N, part, :]
            ext[f, pl.ds(2 * rows, rows), right] = jnp.where(near, halo[NE, part, :], halo[NW, part, :])

    @pl.when(top)
    def _():
        hop_next(1, 4 * rows)
        hop_start(2, 4 * rows)

    @pl.when(relay)
    def _():
        hop_next(1, depth)
        hop_start(2, depth)

    trac_wait(halo_lon.at[0], trac_recv.at[2])
    trac_wait(halo_lon.at[1], trac_recv.at[3])

    @pl.when(jnp.logical_not(top))
    def _():
        trac_wait(halo_lat.at[0], trac_recv.at[0])

    @pl.when(jnp.logical_not(bottom))
    def _():
        trac_wait(halo_lat.at[1], trac_recv.at[1])

    even = (lane8 & 1) == 0
    h_east_tile = halo[E, pl.ds(3 * rows, rows), :]
    h_west_tile = halo[W, pl.ds(3 * rows, rows), :]
    h_north_row = halo[N, pl.ds(3 * rows, 1), :]
    h_south_row = halo[S, pl.ds(4 * rows - 1, 1), :]

    def swap(from_east, from_west):
        return jnp.where(
            even, pltpu.roll(from_east, cols - 1, axis=1), pltpu.roll(from_west, 1, axis=1)
        )

    pt = edge_lon[pl.ds(0, 8), :]
    pu = edge_lon[pl.ds(8, 8), :]
    th = swap(halo_lon[0, pl.ds(0, 8), :], halo_lon[1, pl.ds(0, 8), :])
    uh = swap(halo_lon[0, pl.ds(8, 8), :], halo_lon[1, pl.ds(8, 8), :])

    def column(tile, at):
        lo = jnp.broadcast_to(tile[0:8, at : at + 1], (8, cols))
        hi = jnp.broadcast_to(tile[8:16, at : at + 1], (8, cols))
        return jnp.where(half < depth, lo, hi)

    level_of = (half & (depth - 1)).astype(jnp.float32)
    h_in = jnp.where(even, column(h_own, cols - 1), column(h_own, 0))
    h_out = jnp.where(even, column(h_east_tile, 0), column(h_west_tile, cols - 1))
    wet_pair = (level_of < h_in).astype(jnp.float32) * (level_of < h_out).astype(jnp.float32)

    def lane_mix(l, acc):
        return jnp.where((half & (depth - 1)) == jnp.full((8, cols), l, jnp.int32), horiz[l], acc)

    mix_lanes = lax.fori_loop(0, depth, lane_mix, jnp.zeros((8, cols), jnp.float32), unroll=4)
    signed = jnp.where(even, th - pt, pt - th)
    side_flux = wet_pair * (mix_lanes * signed - 0.25 * (pu + uh) * (pt + th))

    level_row = lax.broadcasted_iota(jnp.int32, (depth, cols), 0).astype(jnp.float32)

    def row_face(low_t, low_v, high_t, high_v, h_low, h_high):
        wet = (level_row < h_low).astype(jnp.float32) * (level_row < h_high).astype(jnp.float32)
        return wet * (mix_rows[...] * (high_t - low_t) - 0.25 * (low_v + high_v) * (low_t + high_t))

    first, second = pl.ds(0, depth), pl.ds(depth, depth)
    face_lat[0] = row_face(
        edge_lat[0, first, :], edge_lat[0, second, :], halo_lat[0, first, :], halo_lat[0, second, :],
        own[pl.ds(4 * rows - 1, 1), :], h_north_row,
    )
    face_lat[1] = row_face(
        halo_lat[1, first, :], halo_lat[1, second, :], edge_lat[1, first, :], edge_lat[1, second, :],
        h_south_row, own[pl.ds(3 * rows, 1), :],
    )

    last_col = lane16 == cols - 1
    first_col = lane16 == 0
    last_row = row16 == rows - 1
    first_row = row16 == 0
    h_e = pltpu.roll(h_own, cols - 1, axis=1)
    h_n = pltpu.roll(h_own, rows - 1, axis=0)

    def fluxes(l, carry):
        at = pl.ds(pl.multiple_of(l * rows, rows), rows)
        t = tr[at, :]
        u = vel[at, :]
        v = vel[pl.ds(pl.multiple_of(v_base + l * rows, rows), rows), :]
        m = horiz[l]
        level = jnp.full((rows, cols), l.astype(jnp.float32))
        wet = (level < h_own).astype(jnp.float32)
        wet_e = (level < h_e).astype(jnp.float32)
        wet_n = (level < h_n).astype(jnp.float32)
        t_e = pltpu.roll(t, cols - 1, axis=1)
        u_e = pltpu.roll(u, cols - 1, axis=1)
        f_e = wet * wet_e * (m * (t_e - t) - 0.25 * (u + u_e) * (t + t_e))
        rim = jnp.concatenate(
            [
                pltpu.roll(side_flux, cols - 1 - 2 * l, axis=1),
                pltpu.roll(side_flux, lax.rem(2 * cols - 1 - 2 * (l + depth), cols), axis=1),
            ],
            axis=0,
        )
        f_e = jnp.where(last_col, rim, f_e)
        f_w = jnp.where(first_col, rim, pltpu.roll(f_e, 1, axis=1))
        t_n = pltpu.roll(t, rows - 1, axis=0)
        v_n = pltpu.roll(v, rows - 1, axis=0)
        f_n = wet * wet_n * (m * (t_n - t) - 0.25 * (v + v_n) * (t + t_n))
        f_n = jnp.where(last_row, face_lat[0, pl.ds(l, 1), :], f_n)
        f_s = jnp.where(first_row, face_lat[1, pl.ds(l, 1), :], pltpu.roll(f_n, 1, axis=0))
        step_ref[at, :] = wet * (t + ((f_e - f_w) + (f_n - f_s)))
        return carry

    lax.fori_loop(0, depth, fluxes, 0, unroll=4)

    def forward(l, sweep):
        at = pl.ds(pl.multiple_of(l * rows, rows), rows)
        sweep = (step_ref[at, :] + cpl[at, :] * sweep) * rec[at, :]
        step_ref[at, :] = sweep
        return sweep

    lax.fori_loop(0, depth, forward, zero, unroll=4)

    def backward(i, x):
        l = depth - 1 - i
        at = pl.ds(pl.multiple_of(l * rows, rows), rows)
        x = step_ref[at, :] - prime[at, :] * x
        tracer_out[at, :] = x
        return x

    lax.fori_loop(0, depth, backward, zero, unroll=4)

    def final_copy(i, size, dst, recv):
        return remote(
            slab.at[3, pl.ds(0, size)],
            dst,
            fin_send.at[i],
            recv,
            {"lat": n_lat - 1, "lon": lon_at(REACH[i])},
        )

    @pl.when(top)
    def _():
        hop_next(2, 4 * rows)
        for i, e in enumerate(REACH):
            if e:
                final_copy(i, 4 * rows, fin.at[i], fin_recv.at[i]).start()

    @pl.when(is_t_relay)
    def _():
        hop_next(2, depth)
        for i in range(len(REACH)):
            final_copy(i, depth, tfin.at[0, i], tfin_recv.at[0, i]).start()

    @pl.when(is_v_relay)
    def _():
        hop_next(2, depth)
        for i in range(len(REACH)):
            final_copy(i, depth, tfin.at[1, i], tfin_recv.at[1, i]).start()

    def source(e):
        m = lon_at(-e)
        sigma = q_odd - m + 1 - 2 * (turn(m) & 1)
        return (sigma + 2 * n_lon) & (n_lon - 1)

    sources = [source(e) for e in REACH]

    def source_of(shape, shift, isu):
        s = lax.broadcasted_iota(jnp.int32, shape, 1)
        l = (jnp.full(shape, r, jnp.int32) - isu - s) & (cols - 1)
        return s, l

    @pl.when(top)
    def _():
        for i, e in enumerate(REACH):
            if e:
                final_copy(i, 4 * rows, fin.at[i], fin_recv.at[i]).wait_recv()
        shape = (4 * rows, cols)
        row = lax.broadcasted_iota(jnp.int32, shape, 0)
        isu = ((row >= rows) & (row < 2 * rows)).astype(jnp.int32)
        s, l = source_of(shape, 0, isu)
        whole = n_lon * cols
        base = jnp.full(shape, pivot_col - lon * cols + 2 * whole, jnp.int32) - isu
        dev_main = ((base - l) & (whole - 1)) >> 7
        off = jnp.where(l < cols // 2, cols, -cols)
        dev_side = ((base - l - off) & (whole - 1)) >> 7
        main = zeros_tile
        side = zeros_tile
        for i, e in enumerate(REACH):
            got = fin[i] if e else slab[3]
            src = jnp.full(shape, sources[i], jnp.int32)
            main = jnp.where(dev_main == src, got, main)
            side = jnp.where(dev_side == src, got, side)
        main = jnp.take_along_axis(main, l, axis=1)
        side = jnp.take_along_axis(side, l, axis=1)
        for f in range(4):
            ff = (0, 1, 3, 2)[f]
            ext[ff, pl.ds(2 * rows, rows), left] = main[f * rows : (f + 1) * rows]
            ext[ff, pl.ds(2 * rows, rows), right] = side[f * rows : (f + 1) * rows]
        fold_fix[pl.ds(0, 1), left] = main[3 * rows + 12 : 3 * rows + 13] - ext[2, pl.ds(2 * rows - 1, 1), left]
        fold_fix[pl.ds(0, 1), right] = side[3 * rows + 12 : 3 * rows + 13] - ext[2, pl.ds(2 * rows - 1, 1), right]

    wide = 2 * cols
    tall = 3 * rows
    h = ext[3]
    sea = (h > 0.0).astype(jnp.float32)

    def east(x):
        return pltpu.roll(x, wide - 1, axis=1)

    def north(x):
        return pltpu.roll(x, tall - 1, axis=0)

    zonal_mask = sea * east(sea)
    merid_mask = sea * north(sea)
    coef[0] = fb_step * ((h + east(h)) / (2.0 * depth)) * zonal_mask
    coef[1] = (1.0 - drag_rate) * zonal_mask
    coef[2] = fb_step * ((h + north(h)) / (2.0 * depth)) * merid_mask
    coef[3] = (1.0 - drag_rate) * merid_mask
    coef[4] = fb_step * sea
    fix_decay = pltpu.roll(coef[3], 1, axis=0)[2 * rows : 2 * rows + 8]

    def cycle(i, state):
        eta, u, v, fix = state
        v_south = pltpu.roll(v, 1, axis=0)
        v_south = jnp.concatenate(
            [v_south[: 2 * rows], v_south[2 * rows : 2 * rows + 8] + fix, v_south[2 * rows + 8 :]], axis=0
        )
        div = (u - pltpu.roll(u, 1, axis=1)) + (v - v_south)
        eta = eta - coef[4] * div
        u = u * coef[1] - coef[0] * (east(eta) - eta)
        v = v * coef[3] - coef[2] * (north(eta) - eta)
        return eta, u, v, fix * fix_decay

    eta, u, v, _ = lax.fori_loop(0, SUB, cycle, (ext[0] * sea, ext[1], ext[2], fold_fix[...]))
    surface_out[...] = eta[rows : 2 * rows, :cols]
    transport_out[pl.ds(0, rows), :] = u[rows : 2 * rows, :cols]
    transport_out[pl.ds(rows, rows), :] = v[rows : 2 * rows, :cols]

    @pl.when(top)
    def _():
        got = []
        for j in range(2):
            shape = (depth, cols)
            s, l = source_of(shape, 0, 0)
            whole = n_lon * cols
            dev = ((jnp.full(shape, pivot_col - lon * cols + 2 * whole, jnp.int32) - l) & (whole - 1)) >> 7
            acc = jnp.zeros(shape, jnp.float32)
            for i in range(len(REACH)):
                trac_wait(tfin.at[j, i], tfin_recv.at[j, i])
                acc = jnp.where(dev == jnp.full(shape, sources[i], jnp.int32), tfin[j, i], acc)
            got.append(jnp.take_along_axis(acc, l, axis=1))
        h_last = own[pl.ds(4 * rows - 1, 1), :]
        flux = row_face(
            edge_lat[0, first, :], edge_lat[0, second, :], got[0], got[1], h_last, ext[3, pl.ds(2 * rows, 1), left]
        )
        face_lat[0] = (level_row < h_last).astype(jnp.float32) * flux
        c_last = cpl[pl.ds(rows - 1, depth, stride=rows), :]
        r_last = rec[pl.ds(rows - 1, depth, stride=rows), :]
        p_last = prime[pl.ds(rows - 1, depth, stride=rows), :]
        out_last = tracer_out[pl.ds(rows - 1, depth, stride=rows), :]
        delta = face_lat[0]
        sweeps = []
        x = jnp.zeros((1, cols), jnp.float32)
        for k in range(depth):
            x = (delta[k : k + 1] + c_last[k : k + 1] * x) * r_last[k : k + 1]
            sweeps.append(x)
        x = jnp.zeros((1, cols), jnp.float32)
        for k in range(depth - 1, -1, -1):
            x = sweeps[k] - p_last[k : k + 1] * x
            tracer_out[pl.ds(k * rows + rows - 1, 1), :] = out_last[k : k + 1] + x

    for side in (E, W):
        halo_copy(side).wait_send()
    lon_copy(True).wait_send()
    lon_copy(False).wait_send()

    @pl.when(jnp.logical_not(top))
    def _():
        for side in (N, NE, NW):
            halo_copy(side).wait_send()
        lat_copy(True).wait_send()

    @pl.when(jnp.logical_not(bottom))
    def _():
        for side in (S, SE, SW):
            halo_copy(side).wait_send()
        lat_copy(False).wait_send()

    @pl.when(top)
    def _():
        spread_copy(0).wait_send()
        spread_copy(1).wait_send()
        for k in range(3):
            for copy in hop_copies(k, 4 * rows):
                copy.wait_send()
        for i, e in enumerate(REACH):
            if e:
                final_copy(i, 4 * rows, fin.at[i], fin_recv.at[i]).wait_send()

    @pl.when(relay)
    def _():
        for k in range(3):
            for copy in hop_copies(k, depth):
                copy.wait_send()
        for i in range(len(REACH)):
            final_copy(i, depth, tfin.at[0, i], tfin_recv.at[0, i]).wait_send()


def solution(mesh):
    n_lon, n_lat = mesh.shape["lon"], mesh.shape["lat"]

    def shards(tracer, velocity, surface, transport, horiz_mixing, vert_mixing, levels, land_tiles, fold_pair):
        depth, rows, cols = tracer.shape
        f32 = jnp.float32
        hbm = pl.BlockSpec(memory_space=pl.ANY)
        smem = pl.BlockSpec(memory_space=pltpu.SMEM)
        vmem = pl.BlockSpec(memory_space=pltpu.VMEM)
        dma = pltpu.SemaphoreType.DMA
        field = pltpu.VMEM((depth * rows, cols), f32)
        tracer_new, surface_new, transport_new = pl.pallas_call(
            functools.partial(ocean_kernel, n_lon, n_lat, depth, rows, cols),
            name="ocean",
            out_shape=(
                jax.ShapeDtypeStruct((depth * rows, cols), f32),
                jax.ShapeDtypeStruct((rows, cols), f32),
                jax.ShapeDtypeStruct((2 * rows, cols), f32),
            ),
            in_specs=[hbm] * 5 + [smem] * 4,
            out_specs=(vmem, vmem, vmem),
            scratch_shapes=[
                field,
                pltpu.VMEM((2 * depth * rows, cols), f32),
                pltpu.VMEM((rows, cols), jnp.int32),
                pltpu.VMEM((4 * rows, cols), f32),
                pltpu.VMEM((8, 4 * rows, cols), f32),
                pltpu.VMEM((16, cols), f32),
                pltpu.VMEM((2, 16, cols), f32),
                pltpu.VMEM((2, 2 * depth, cols), f32),
                pltpu.VMEM((2, 2 * depth, cols), f32),
                pltpu.VMEM((4, 4 * rows, cols), f32),
                pltpu.VMEM((6, 4 * rows, cols), f32),
                pltpu.VMEM((7, 4 * rows, cols), f32),
                pltpu.VMEM((2, 7, depth, cols), f32),
                field,
                field,
                field,
                field,
                pltpu.VMEM((2, depth, cols), f32),
                pltpu.VMEM((depth, cols), f32),
                pltpu.VMEM((4, 3 * rows, 2 * cols), f32),
                pltpu.VMEM((5, 3 * rows, 2 * cols), f32),
                pltpu.VMEM((8, 2 * cols), f32),
                dma((5,)),
                dma((8,)),
                dma((8,)),
                dma((6,)),
                dma((5,)),
                dma((6,)),
                dma((6,)),
                dma((7,)),
                dma((7,)),
                dma((2, 7)),
            ],
            compiler_params=pltpu.CompilerParams(collective_id=1, has_side_effects=True),
        )(
            tracer.reshape(depth * rows, cols),
            velocity.reshape(2 * depth * rows, cols),
            surface,
            transport.reshape(2 * rows, cols),
            levels,
            horiz_mixing,
            vert_mixing,
            land_tiles,
            fold_pair,
        )
        return (
            tracer_new.reshape(depth, rows, cols),
            surface_new,
            transport_new.reshape(2, rows, cols),
        )

    return jax.shard_map(
        shards,
        mesh=mesh,
        in_specs=(
            P("member", "lat", "lon"),
            P(None, "member", "lat", "lon"),
            P(("member", "lat"), "lon"),
            P("member", "lat", "lon"),
            P("member"),
            P("member"),
            P("lat", "lon"),
            P("lat", "lon"),
            P("lon"),
        ),
        out_specs=(
            P("member", "lat", "lon"),
            P(("member", "lat"), "lon"),
            P("member", "lat", "lon"),
        ),
        check_vma=False,
    )
```

```python
import functools

import jax
import jax.numpy as jnp
from jax import lax
from jax.experimental import pallas as pl
from jax.experimental.pallas import tpu as pltpu
from jax.sharding import PartitionSpec as P

SUB = 12
fb_step = 0.6
drag_rate = 0.02
MESH = pl.DeviceIdType.MESH

E, W, N, S, NE, NW, SE, SW = range(8)
OPPOSITE = {E: W, W: E, N: S, S: N, NE: SW, SW: NE, NW: SE, SE: NW}
STEP = {E: (0, 1), W: (0, -1), N: (1, 0), S: (-1, 0), NE: (1, 1), NW: (1, -1), SE: (-1, 1), SW: (-1, -1)}
GROUP = 4


def ocean_kernel(
    n_lon,
    n_lat,
    depth,
    rows,
    cols,
    tracer_hbm,
    velocity_hbm,
    surface_hbm,
    transport_hbm,
    levels_hbm,
    horiz_hbm,
    vert_hbm,
    land_hbm,
    fold_hbm,
    tracer_out,
    surface_out,
    transport_out,
    horiz,
    vert,
    land,
    fold,
    tr,
    vel,
    lev,
    own,
    halo,
    side_out,
    side_in,
    edge_lon,
    halo_lon,
    edge_lat,
    halo_lat,
    slab,
    hold,
    fwd_out,
    fwd_in,
    pick,
    fin,
    tfin,
    step_ref,
    cpl,
    rec,
    prime,
    face_lat,
    mix_rows,
    ext,
    coef,
    fold_fix,
    load_sem,
    halo_send,
    halo_recv,
    trac_send,
    trac_recv,
    hold_send,
    hold_recv,
    fwd_send,
    fwd_recv,
    fin_send,
    fin_recv,
    tfin_recv,
):
    lat = lax.axis_index("lat")
    lon = lax.axis_index("lon")
    top = lat == n_lat - 1
    bottom = lat == 0
    t_relay = n_lat - 3
    v_relay = 1
    is_t_relay = lat == t_relay
    is_v_relay = lat == v_relay
    relay = is_t_relay | is_v_relay
    ring = top | relay
    n_group = n_lon // GROUP
    me = lon & (GROUP - 1)
    group = lon - me
    keeper = lon < GROUP
    half_way = n_group // 2
    at_group = lon >> 2
    rising = at_group <= half_way
    blocks = jnp.where(rising, half_way + 2 - at_group, half_way + 1 - n_group + at_group)
    onward = jnp.where(rising, GROUP, -GROUP)
    has_next = jnp.logical_not(keeper) & (blocks > 2)
    has_previous = (at_group > 1) & (at_group < n_group - 1)

    def partner(g):
        return g * GROUP + (GROUP - 1 - me)

    def lon_at(step):
        return lax.rem(lon + step + n_lon, n_lon)

    def lat_at(step):
        return lax.rem(lat + step + n_lat, n_lat)

    def remote(src, dst, send, recv, to):
        return pltpu.make_async_remote_copy(
            src_ref=src, dst_ref=dst, send_sem=send, recv_sem=recv, device_id=to, device_id_type=MESH
        )

    small = [
        pltpu.make_async_copy(surface_hbm, own.at[pl.ds(0, rows)], load_sem.at[0]),
        pltpu.make_async_copy(transport_hbm, own.at[pl.ds(rows, 2 * rows)], load_sem.at[1]),
        pltpu.make_async_copy(levels_hbm, lev, load_sem.at[2]),
        pltpu.make_async_copy(land_hbm, land, load_sem.at[5]),
        pltpu.make_async_copy(fold_hbm, fold, load_sem.at[6]),
        pltpu.make_async_copy(horiz_hbm, horiz, load_sem.at[7]),
        pltpu.make_async_copy(vert_hbm, vert, load_sem.at[8]),
    ]
    large = [
        pltpu.make_async_copy(tracer_hbm, tr, load_sem.at[3]),
        pltpu.make_async_copy(velocity_hbm, vel, load_sem.at[4]),
    ]
    for copy in small:
        copy.start()
    barrier = pltpu.get_barrier_semaphore()
    peers = [STEP[side] for side in range(8)] + [(2, 0), (-2, 0)]
    for d_lat, d_lon in peers:
        pl.semaphore_signal(
            barrier, inc=1, device_id={"lat": lat_at(d_lat), "lon": lon_at(d_lon)}, device_id_type=MESH
        )

    @pl.when(ring)
    def _():
        @pl.when(keeper)
        def _():
            for g in range(1, n_group):
                pl.semaphore_signal(barrier, inc=1, device_id={"lon": partner(g)}, device_id_type=MESH)

        @pl.when(has_previous)
        def _():
            pl.semaphore_signal(barrier, inc=1, device_id={"lon": lon - onward}, device_id_type=MESH)

        for e in range(1, GROUP):
            pl.semaphore_signal(
                barrier, inc=1, device_id={"lon": group + ((me + e) & (GROUP - 1))}, device_id_type=MESH
            )

    for copy in large:
        copy.start()

    zeros_tile = jnp.zeros((4 * rows, cols), jnp.float32)

    @pl.when(bottom)
    def _():
        halo[1] = zeros_tile
        for side in (SE, SW):
            side_in[side] = jnp.zeros((8, cols), jnp.float32)
        halo_lat[1] = jnp.zeros((2 * depth, cols), jnp.float32)

    @pl.when(top)
    def _():
        halo[0] = zeros_tile
        for side in (NE, NW):
            side_in[side] = jnp.zeros((8, cols), jnp.float32)
        halo_lat[0] = jnp.zeros((2 * depth, cols), jnp.float32)

    for copy in small:
        copy.wait()
    dry = 1 - land[0, 0]
    own[pl.ds(3 * rows, rows), :] = (lev[...] * dry).astype(jnp.float32)

    lane8 = lax.broadcasted_iota(jnp.int32, (8, cols), 1)
    to_east, to_west = jnp.zeros((8, cols), jnp.float32), jnp.zeros((8, cols), jnp.float32)
    for k in range(8):
        here = (lane8 >> 4) == k
        part = own[pl.ds(8 * k, 8), :]
        to_east = jnp.where(here, pltpu.roll(part, (16 * k + 16) % cols, axis=1), to_east)
        to_west = jnp.where(here, pltpu.roll(part, 16 * k, axis=1) if k else part, to_west)
    side_out[0] = to_east
    side_out[1] = to_west

    @pl.when(top)
    def _():
        slab[...] = zeros_tile
        for i in range(12):
            last = rows - 1 - i
            slab[pl.ds(i, 1), :] = own[pl.ds(last, 1), :]
            slab[pl.ds(rows + i, 1), :] = -own[pl.ds(rows + last, 1), :]
            slab[pl.ds(2 * rows + i, 1), :] = own[pl.ds(3 * rows + last, 1), :]
            slab[pl.ds(3 * rows + i, 1), :] = -own[pl.ds(2 * rows + last - 1, 1), :]
        slab[pl.ds(3 * rows + 12, 1), :] = -own[pl.ds(3 * rows - 1, 1), :]

    pl.semaphore_wait(barrier, len(peers) + jnp.where(ring, GROUP - jnp.where(keeper, 1, 0) + jnp.where(has_next, 1, 0), 0))

    pivot_col = lax.rem(fold[0] + lon * cols, n_lon * cols)
    q = lax.div(pivot_col, cols)
    r = lax.rem(pivot_col, cols)

    def halo_copy(side):
        d_lat, d_lon = STEP[side]
        slot = OPPOSITE[side]
        if d_lon == 0:
            src, dst = own, halo.at[0 if slot == N else 1]
        else:
            src, dst = side_out.at[0 if d_lon == 1 else 1], side_in.at[slot]
        return remote(
            src,
            dst,
            halo_send.at[side],
            halo_recv.at[slot],
            {"lat": lat_at(d_lat), "lon": lon_at(d_lon)},
        )

    def halo_wait(side):
        dst = halo.at[0 if side == N else 1] if side in (N, S) else side_in.at[side]
        remote(dst, dst, halo_send.at[side], halo_recv.at[side], {"lon": lon}).wait_recv()

    for side in (E, W):
        halo_copy(side).start()

    @pl.when(jnp.logical_not(top))
    def _():
        for side in (N, NE, NW):
            halo_copy(side).start()

    @pl.when(jnp.logical_not(bottom))
    def _():
        for side in (S, SE, SW):
            halo_copy(side).start()

    def hold_copy(size):
        slot = lon >> 2
        return remote(
            slab.at[pl.ds(0, size)],
            hold.at[slot, pl.ds(0, size)],
            hold_send.at[0],
            hold_recv.at[slot],
            {"lon": partner(0)},
        )

    def wanted(kind, to):
        low = q - to - 2 + 2 * n_lon
        return (low + ((kind - low) & (GROUP - 1))) & (n_lon - 1)

    def kind_of(place):
        return jnp.where(keeper, GROUP - 1 - place, place)

    def lowest(kind, g):
        return wanted(kind, g * GROUP + GROUP - 1) >> 2

    @pl.when(top)
    def _():
        hold_copy(4 * rows).start()

    for copy in large:
        copy.wait()
    u_base = 0
    v_base = depth * rows
    edge_lat[0, pl.ds(0, depth), :] = tr[pl.ds(rows - 1, depth, stride=rows), :]
    edge_lat[0, pl.ds(depth, depth), :] = vel[pl.ds(v_base + rows - 1, depth, stride=rows), :]
    edge_lat[1, pl.ds(0, depth), :] = tr[pl.ds(0, depth, stride=rows), :]
    edge_lat[1, pl.ds(depth, depth), :] = vel[pl.ds(v_base, depth, stride=rows), :]

    def spread_copy(j):
        to = (t_relay, v_relay)[j]
        return remote(
            edge_lat.at[0, pl.ds(j * depth, depth)],
            slab.at[pl.ds(0, depth)],
            trac_send.at[j],
            trac_recv.at[4],
            {"lat": to},
        )

    def lat_copy(north):
        slot = 1 if north else 0
        return remote(
            edge_lat.at[0 if north else 1],
            halo_lat.at[slot],
            trac_send.at[0 if north else 2],
            trac_recv.at[slot],
            {"lat": lat_at(1 if north else -1)},
        )

    @pl.when(top)
    def _():
        spread_copy(0).start()
        spread_copy(1).start()

    @pl.when(jnp.logical_not(top))
    def _():
        lat_copy(True).start()

    @pl.when(jnp.logical_not(bottom))
    def _():
        lat_copy(False).start()

    half = lane8 >> 1

    def pack(l, carry):
        pt, pu = carry
        for g in range(2):
            item = l + depth * g
            here = half == jnp.full((8, cols), item, jnp.int32)
            at = pl.multiple_of(l * rows + 8 * g, 8)
            pt = jnp.where(here, pltpu.roll(tr[pl.ds(at, 8), :], 2 * item + 1, axis=1), pt)
            pu = jnp.where(here, pltpu.roll(vel[pl.ds(at, 8), :], 2 * item + 1, axis=1), pu)
        return pt, pu

    pt, pu = lax.fori_loop(
        0, depth, pack, (jnp.zeros((8, cols), jnp.float32), jnp.zeros((8, cols), jnp.float32)), unroll=4
    )
    edge_lon[pl.ds(0, 8), :] = pt
    edge_lon[pl.ds(8, 8), :] = pu

    def lon_copy(east):
        slot = 1 if east else 0
        return remote(
            edge_lon,
            halo_lon.at[slot],
            trac_send.at[3 if east else 4],
            trac_recv.at[2 + slot],
            {"lon": lon_at(1 if east else -1)},
        )

    lon_copy(True).start()
    lon_copy(False).start()


    def trac_wait(dst, sem):
        remote(dst, dst, trac_send.at[5], sem, {"lon": lon}).wait_recv()

    @pl.when(relay)
    def _():
        trac_wait(slab.at[pl.ds(0, depth)], trac_recv.at[4])
        hold_copy(depth).start()

    h_own = own[pl.ds(3 * rows, rows), :]

    def pivots(l, carry):
        c_up, p_up = carry
        wet_below = (jnp.full((rows, cols), (l + 1).astype(jnp.float32)) < h_own).astype(jnp.float32)
        c_down = vert[jnp.minimum(l, depth - 2)] * wet_below
        pivot = (1.0 + c_up + c_down) + c_up * p_up
        inv = 1.0 / pivot
        p_down = -c_down * inv
        at = pl.ds(pl.multiple_of(l * rows, rows), rows)
        cpl[at, :] = c_up
        rec[at, :] = inv
        prime[at, :] = p_down
        mix_rows[pl.ds(l, 1), :] = jnp.full((1, cols), horiz[l])
        return c_down, p_down

    zero = jnp.zeros((rows, cols), jnp.float32)
    lax.fori_loop(0, depth, pivots, (zero, zero), unroll=2)

    lane16 = lax.broadcasted_iota(jnp.int32, (rows, cols), 1)
    row16 = lax.broadcasted_iota(jnp.int32, (rows, cols), 0)
    last_col = lane16 == cols - 1
    first_col = lane16 == 0
    last_row = row16 == rows - 1
    first_row = row16 == 0
    h_e = jnp.where(last_col, 0.0, pltpu.roll(h_own, cols - 1, axis=1))
    h_n = jnp.where(last_row, 0.0, pltpu.roll(h_own, rows - 1, axis=0))

    def fluxes(l, carry):
        at = pl.ds(pl.multiple_of(l * rows, rows), rows)
        t = tr[at, :]
        u = vel[at, :]
        v = vel[pl.ds(pl.multiple_of(v_base + l * rows, rows), rows), :]
        m = horiz[l]
        level = jnp.full((rows, cols), l.astype(jnp.float32))
        wet = (level < h_own).astype(jnp.float32)
        wet_e = (level < h_e).astype(jnp.float32)
        wet_n = (level < h_n).astype(jnp.float32)
        t_e = pltpu.roll(t, cols - 1, axis=1)
        u_e = pltpu.roll(u, cols - 1, axis=1)
        f_e = wet * wet_e * (m * (t_e - t) - 0.25 * (u + u_e) * (t + t_e))
        f_w = pltpu.roll(f_e, 1, axis=1)
        t_n = pltpu.roll(t, rows - 1, axis=0)
        v_n = pltpu.roll(v, rows - 1, axis=0)
        f_n = wet * wet_n * (m * (t_n - t) - 0.25 * (v + v_n) * (t + t_n))
        f_s = pltpu.roll(f_n, 1, axis=0)
        step_ref[at, :] = wet * (t + ((f_e - f_w) + (f_n - f_s)))
        return carry

    lax.fori_loop(0, depth, fluxes, 0, unroll=4)

    def final_copy(e, size, dst, recv):
        return remote(
            pick.at[e, pl.ds(0, size)], dst, fin_send.at[e], recv, {"lat": n_lat - 1, "lon": group + e}
        )

    def forward_copy(out, slot, to, size):
        return remote(
            fwd_out.at[out, pl.ds(0, size)], fwd_in.at[slot, pl.ds(0, size)], fwd_send.at[out], fwd_recv.at[slot], {"lon": to}
        )

    def chain_copy(slot, size):
        return remote(
            fwd_in.at[slot, pl.ds(0, size)],
            fwd_in.at[slot - 1, pl.ds(0, size)],
            fwd_send.at[slot],
            fwd_recv.at[slot - 1],
            {"lon": lon + onward},
        )

    def chain_wait(slot, size):
        dst = fwd_in.at[slot, pl.ds(0, size)]
        remote(dst, dst, fwd_send.at[0], fwd_recv.at[slot], {"lon": partner(0)}).wait_recv()

    rise, fall = half_way + 1, half_way

    def serve(size, block, target):
        def send(e, carry):
            pick[e, pl.ds(0, size), :] = block(e)
            target(e)
            return carry

        lax.fori_loop(0, GROUP, send, 0)

    def to_top(e):
        @pl.when(e != me)
        def _():
            final_copy(e, 4 * rows, fin.at[me], fin_recv.at[me]).start()

    def to_relayed(j):
        return lambda e: final_copy(e, depth, tfin.at[j, me], tfin_recv.at[j, me]).start()

    members = ((top, 4 * rows, to_top), (is_t_relay, depth, to_relayed(0)), (is_v_relay, depth, to_relayed(1)))

    for role, size, target in members:

        @pl.when(role & keeper)
        def _(size=size, target=target):
            for g in range(n_group):
                dst = hold.at[g, pl.ds(0, size)]
                remote(dst, dst, hold_send.at[0], hold_recv.at[g], {"lon": partner(0)}).wait_recv()
            serve(size, lambda e: hold[wanted(GROUP - 1 - me, e) >> 2, pl.ds(0, size), :], target)

            first_up = lowest(GROUP - 1 - me, 1)
            first_down = lowest(GROUP - 1 - me, n_group - 1)

            def forward_up(j, carry):
                slot = (first_up + 1 - j + n_group) & (n_group - 1)
                fwd_out[j, pl.ds(0, size), :] = hold[slot, pl.ds(0, size), :]
                forward_copy(j, j, partner(1), size).start()
                return carry

            def forward_down(j, carry):
                slot = (first_down + j) & (n_group - 1)
                fwd_out[rise + j, pl.ds(0, size), :] = hold[slot, pl.ds(0, size), :]
                forward_copy(rise + j, j, partner(n_group - 1), size).start()
                return carry

            lax.fori_loop(0, rise, forward_up, 0)
            lax.fori_loop(0, fall, forward_down, 0)

    for side in (E, W):
        halo_wait(side)

    @pl.when(jnp.logical_not(top))
    def _():
        for side in (N, NE, NW):
            halo_wait(side)

    @pl.when(jnp.logical_not(bottom))
    def _():
        for side in (S, SE, SW):
            halo_wait(side)

    near = lane8 < cols // 2
    west_half, east_half = pl.ds(0, cols), pl.ds(cols, cols)

    def beside(east, west, base):
        for k in range(8):
            tile = jnp.where(
                near,
                pltpu.roll(side_in[east], (cols - 16 * k) % cols, axis=1),
                pltpu.roll(side_in[west], (cols - 16 - 16 * k) % cols, axis=1),
            )
            ext[k // 2, pl.ds(base + 8 * (k % 2), 8), east_half] = tile

    beside(SE, SW, 0)
    beside(E, W, rows)
    for f in range(4):
        part = pl.ds(f * rows, rows)
        ext[f, pl.ds(0, rows), west_half] = halo[1, part, :]
        ext[f, pl.ds(rows, rows), west_half] = own[part, :]
    fold_fix[...] = jnp.zeros((8, 2 * cols), jnp.float32)

    @pl.when(jnp.logical_not(top))
    def _():
        beside(NE, NW, 2 * rows)
        for f in range(4):
            ext[f, pl.ds(2 * rows, rows), west_half] = halo[0, pl.ds(f * rows, rows), :]

    trac_wait(halo_lon.at[0], trac_recv.at[2])
    trac_wait(halo_lon.at[1], trac_recv.at[3])

    @pl.when(jnp.logical_not(top))
    def _():
        trac_wait(halo_lat.at[0], trac_recv.at[0])

    @pl.when(jnp.logical_not(bottom))
    def _():
        trac_wait(halo_lat.at[1], trac_recv.at[1])

    even = (lane8 & 1) == 0
    h_beside = ext[3, pl.ds(rows, rows), east_half]
    h_north_row = halo[0, pl.ds(3 * rows, 1), :]
    h_south_row = halo[1, pl.ds(4 * rows - 1, 1), :]

    def swap(from_east, from_west):
        return jnp.where(
            even, pltpu.roll(from_east, cols - 1, axis=1), pltpu.roll(from_west, 1, axis=1)
        )

    pt = edge_lon[pl.ds(0, 8), :]
    pu = edge_lon[pl.ds(8, 8), :]
    th = swap(halo_lon[0, pl.ds(0, 8), :], halo_lon[1, pl.ds(0, 8), :])
    uh = swap(halo_lon[0, pl.ds(8, 8), :], halo_lon[1, pl.ds(8, 8), :])

    def column(tile, at):
        lo = jnp.broadcast_to(tile[0:8, at : at + 1], (8, cols))
        hi = jnp.broadcast_to(tile[8:16, at : at + 1], (8, cols))
        return jnp.where(half < depth, lo, hi)

    level_of = (half & (depth - 1)).astype(jnp.float32)
    h_in = jnp.where(even, column(h_own, cols - 1), column(h_own, 0))
    h_out = jnp.where(even, column(h_beside, 0), column(h_beside, cols - 1))
    wet_pair = (level_of < h_in).astype(jnp.float32) * (level_of < h_out).astype(jnp.float32)

    def lane_mix(l, acc):
        return jnp.where((half & (depth - 1)) == jnp.full((8, cols), l, jnp.int32), horiz[l], acc)

    mix_lanes = lax.fori_loop(0, depth, lane_mix, jnp.zeros((8, cols), jnp.float32), unroll=4)
    sign = jnp.where(even, 1.0, -1.0)
    side_flux = wet_pair * (mix_lanes * (th - pt) - sign * (0.25 * (pu + uh) * (pt + th)))

    level_row = lax.broadcasted_iota(jnp.int32, (depth, cols), 0).astype(jnp.float32)

    def row_face(low_t, low_v, high_t, high_v, h_low, h_high):
        wet = (level_row < h_low).astype(jnp.float32) * (level_row < h_high).astype(jnp.float32)
        return wet * (mix_rows[...] * (high_t - low_t) - 0.25 * (low_v + high_v) * (low_t + high_t))

    first, second = pl.ds(0, depth), pl.ds(depth, depth)
    face_lat[0] = row_face(
        edge_lat[0, first, :], edge_lat[0, second, :], halo_lat[0, first, :], halo_lat[0, second, :],
        own[pl.ds(4 * rows - 1, 1), :], h_north_row,
    )
    face_lat[1] = row_face(
        halo_lat[1, first, :], halo_lat[1, second, :], edge_lat[1, first, :], edge_lat[1, second, :],
        h_south_row, own[pl.ds(3 * rows, 1), :],
    )

    rim_col = last_col | first_col

    def forward(l, sweep):
        at = pl.ds(pl.multiple_of(l * rows, rows), rows)
        rim = jnp.concatenate(
            [
                pltpu.roll(side_flux, cols - 1 - 2 * l, axis=1),
                pltpu.roll(side_flux, lax.rem(2 * cols - 1 - 2 * (l + depth), cols), axis=1),
            ],
            axis=0,
        )
        gain = jnp.where(rim_col, rim, 0.0) + (
            jnp.where(last_row, face_lat[0, pl.ds(l, 1), :], 0.0)
            - jnp.where(first_row, face_lat[1, pl.ds(l, 1), :], 0.0)
        )
        sweep = ((step_ref[at, :] + gain) + cpl[at, :] * sweep) * rec[at, :]
        step_ref[at, :] = sweep
        return sweep

    lax.fori_loop(0, depth, forward, zero, unroll=4)

    def backward(i, x):
        l = depth - 1 - i
        at = pl.ds(pl.multiple_of(l * rows, rows), rows)
        x = step_ref[at, :] - prime[at, :] * x
        tracer_out[at, :] = x
        return x

    lax.fori_loop(0, depth, backward, zero, unroll=4)

    for role, size, target in members:

        @pl.when(role & jnp.logical_not(keeper))
        def _(size=size, target=target):
            chain_wait(0, size)
            chain_wait(1, size)

            @pl.when(has_next)
            def _():
                chain_copy(1, size).start()

            first_slot = lowest(me, at_group)
            turned = jnp.where(rising, 1, 0)

            def either(e):
                which = ((wanted(me, group + e) >> 2) - first_slot + turned) & 1
                return jnp.where(
                    jnp.full((size, cols), which, jnp.int32) == 1,
                    fwd_in[1, pl.ds(0, size), :],
                    fwd_in[0, pl.ds(0, size), :],
                )

            serve(size, either, target)

            def hand_on(slot, carry):
                chain_wait(slot, size)
                chain_copy(slot, size).start()
                return carry

            lax.fori_loop(2, blocks, hand_on, 0)

    def source_of(shape, shift, isu):
        s = lax.broadcasted_iota(jnp.int32, shape, 1)
        l = (jnp.full(shape, r, jnp.int32) - isu - s) & (cols - 1)
        return s, l

    @pl.when(top)
    def _():
        shape = (4 * rows, cols)
        row = lax.broadcasted_iota(jnp.int32, shape, 0)
        isu = ((row >= rows) & (row < 2 * rows)).astype(jnp.int32)
        s, l = source_of(shape, 0, isu)
        whole = n_lon * cols
        base = jnp.full(shape, pivot_col - lon * cols + 2 * whole, jnp.int32) - isu
        dev_main = ((base - l) & (whole - 1)) >> 7
        off = jnp.where(l < cols // 2, cols, -cols)
        dev_side = ((base - l - off) & (whole - 1)) >> 7
        main, side = zeros_tile, zeros_tile
        for e in range(GROUP):
            @pl.when(e != me)
            def _():
                trac_wait(fin.at[e], fin_recv.at[e])

            @pl.when(e == me)
            def _():
                fin[e] = pick[e]

        for e in range(GROUP):
            got = fin[e]
            src = jnp.full(shape, wanted(kind_of(e), lon), jnp.int32)
            main = jnp.where(dev_main == src, got, main)
            side = jnp.where(dev_side == src, got, side)
        main = jnp.take_along_axis(main, l, axis=1)
        side = jnp.take_along_axis(side, l, axis=1)
        for f in range(4):
            ff = (0, 1, 3, 2)[f]
            ext[ff, pl.ds(2 * rows, rows), west_half] = main[f * rows : (f + 1) * rows]
            ext[ff, pl.ds(2 * rows, rows), east_half] = side[f * rows : (f + 1) * rows]
        fold_fix[pl.ds(0, 1), west_half] = main[3 * rows + 12 : 3 * rows + 13] - ext[2, pl.ds(2 * rows - 1, 1), west_half]
        fold_fix[pl.ds(0, 1), east_half] = side[3 * rows + 12 : 3 * rows + 13] - ext[2, pl.ds(2 * rows - 1, 1), east_half]

    wide = 2 * cols
    tall = 3 * rows
    h = ext[3]
    sea = (h > 0.0).astype(jnp.float32)

    def east(x):
        return pltpu.roll(x, wide - 1, axis=1)

    def north(x):
        return pltpu.roll(x, tall - 1, axis=0)

    zonal_mask = sea * east(sea)
    merid_mask = sea * north(sea)
    coef[0] = fb_step * ((h + east(h)) / (2.0 * depth)) * zonal_mask
    coef[1] = (1.0 - drag_rate) * zonal_mask
    coef[2] = fb_step * ((h + north(h)) / (2.0 * depth)) * merid_mask
    coef[3] = (1.0 - drag_rate) * merid_mask
    coef[4] = fb_step * sea
    fix_decay = pltpu.roll(coef[3], 1, axis=0)[2 * rows : 2 * rows + 8]

    def cycle(i, state):
        eta, u, v, fix = state
        v_south = pltpu.roll(v, 1, axis=0)
        v_south = jnp.concatenate(
            [v_south[: 2 * rows], v_south[2 * rows : 2 * rows + 8] + fix, v_south[2 * rows + 8 :]], axis=0
        )
        div = (u - pltpu.roll(u, 1, axis=1)) + (v - v_south)
        eta = eta - coef[4] * div
        u = u * coef[1] - coef[0] * (east(eta) - eta)
        v = v * coef[3] - coef[2] * (north(eta) - eta)
        return eta, u, v, fix * fix_decay

    eta, u, v, _ = lax.fori_loop(0, SUB, cycle, (ext[0] * sea, ext[1], ext[2], fold_fix[...]))
    surface_out[...] = eta[rows : 2 * rows, :cols]
    transport_out[pl.ds(0, rows), :] = u[rows : 2 * rows, :cols]
    transport_out[pl.ds(rows, rows), :] = v[rows : 2 * rows, :cols]

    @pl.when(top)
    def _():
        got = []
        for j in range(2):
            shape = (depth, cols)
            s, l = source_of(shape, 0, 0)
            whole = n_lon * cols
            dev = ((jnp.full(shape, pivot_col - lon * cols + 2 * whole, jnp.int32) - l) & (whole - 1)) >> 7
            acc = jnp.zeros(shape, jnp.float32)
            for e in range(GROUP):
                trac_wait(tfin.at[j, e], tfin_recv.at[j, e])
                acc = jnp.where(dev == jnp.full(shape, wanted(kind_of(e), lon), jnp.int32), tfin[j, e], acc)
            got.append(jnp.take_along_axis(acc, l, axis=1))
        h_last = own[pl.ds(4 * rows - 1, 1), :]
        flux = row_face(
            edge_lat[0, first, :], edge_lat[0, second, :], got[0], got[1], h_last, ext[3, pl.ds(2 * rows, 1), west_half]
        )
        face_lat[0] = (level_row < h_last).astype(jnp.float32) * flux
        c_last = cpl[pl.ds(rows - 1, depth, stride=rows), :]
        r_last = rec[pl.ds(rows - 1, depth, stride=rows), :]
        p_last = prime[pl.ds(rows - 1, depth, stride=rows), :]
        out_last = tracer_out[pl.ds(rows - 1, depth, stride=rows), :]
        delta = face_lat[0]
        sweeps = []
        x = jnp.zeros((1, cols), jnp.float32)
        for k in range(depth):
            x = (delta[k : k + 1] + c_last[k : k + 1] * x) * r_last[k : k + 1]
            sweeps.append(x)
        x = jnp.zeros((1, cols), jnp.float32)
        for k in range(depth - 1, -1, -1):
            x = sweeps[k] - p_last[k : k + 1] * x
            tracer_out[pl.ds(k * rows + rows - 1, 1), :] = out_last[k : k + 1] + x

    for side in (E, W):
        halo_copy(side).wait_send()
    lon_copy(True).wait_send()
    lon_copy(False).wait_send()

    @pl.when(jnp.logical_not(top))
    def _():
        for side in (N, NE, NW):
            halo_copy(side).wait_send()
        lat_copy(True).wait_send()

    @pl.when(jnp.logical_not(bottom))
    def _():
        for side in (S, SE, SW):
            halo_copy(side).wait_send()
        lat_copy(False).wait_send()

    @pl.when(top)
    def _():
        spread_copy(0).wait_send()
        spread_copy(1).wait_send()

        hold_copy(4 * rows).wait_send()

        @pl.when(keeper)
        def _():
            for j in range(rise):
                forward_copy(j, j, partner(1), 4 * rows).wait_send()
            for j in range(fall):
                forward_copy(rise + j, j, partner(n_group - 1), 4 * rows).wait_send()

        @pl.when(has_next)
        def _():
            def gone(slot, carry):
                chain_copy(slot, 4 * rows).wait_send()
                return carry

            lax.fori_loop(1, blocks, gone, 0)

        for e in range(GROUP):

            @pl.when(e != me)
            def _(e=e):
                final_copy(e, 4 * rows, fin.at[me], fin_recv.at[me]).wait_send()

    @pl.when(relay)
    def _():
        hold_copy(depth).wait_send()

        @pl.when(keeper)
        def _():
            for j in range(rise):
                forward_copy(j, j, partner(1), depth).wait_send()
            for j in range(fall):
                forward_copy(rise + j, j, partner(n_group - 1), depth).wait_send()

        @pl.when(has_next)
        def _():
            def gone(slot, carry):
                chain_copy(slot, depth).wait_send()
                return carry

            lax.fori_loop(1, blocks, gone, 0)

        for e in range(GROUP):
            final_copy(e, depth, tfin.at[0, me], tfin_recv.at[0, me]).wait_send()


def solution(mesh):
    n_lon, n_lat = mesh.shape["lon"], mesh.shape["lat"]

    def shards(tracer, velocity, surface, transport, horiz_mixing, vert_mixing, levels, land_tiles, fold_pair):
        depth, rows, cols = tracer.shape
        f32 = jnp.float32
        hbm = pl.BlockSpec(memory_space=pl.ANY)
        vmem = pl.BlockSpec(memory_space=pltpu.VMEM)
        dma = pltpu.SemaphoreType.DMA
        field = pltpu.VMEM((depth * rows, cols), f32)
        tracer_new, surface_new, transport_new = pl.pallas_call(
            functools.partial(ocean_kernel, n_lon, n_lat, depth, rows, cols),
            name="ocean",
            out_shape=(
                pltpu.VMEM((depth * rows, cols), f32),
                pltpu.VMEM((rows, cols), f32),
                pltpu.VMEM((2 * rows, cols), f32),
            ),
            in_specs=[hbm] * 9,
            out_specs=(vmem, vmem, vmem),
            scratch_shapes=[
                pltpu.SMEM((depth,), f32),
                pltpu.SMEM((depth - 1,), f32),
                pltpu.SMEM((1, 1), jnp.int32),
                pltpu.SMEM((cols,), jnp.int32),
                field,
                pltpu.VMEM((2 * depth * rows, cols), f32),
                pltpu.VMEM((rows, cols), jnp.int32),
                pltpu.VMEM((4 * rows, cols), f32),
                pltpu.VMEM((2, 4 * rows, cols), f32),
                pltpu.VMEM((2, 8, cols), f32),
                pltpu.VMEM((8, 8, cols), f32),
                pltpu.VMEM((16, cols), f32),
                pltpu.VMEM((2, 16, cols), f32),
                pltpu.VMEM((2, 2 * depth, cols), f32),
                pltpu.VMEM((2, 2 * depth, cols), f32),
                pltpu.VMEM((4 * rows, cols), f32),
                pltpu.VMEM((n_lon // GROUP, 4 * rows, cols), f32),
                pltpu.VMEM((n_lon // GROUP + 1, 4 * rows, cols), f32),
                pltpu.VMEM((n_lon // GROUP // 2 + 1, 4 * rows, cols), f32),
                pltpu.VMEM((GROUP, 4 * rows, cols), f32),
                pltpu.VMEM((GROUP, 4 * rows, cols), f32),
                pltpu.VMEM((2, GROUP, depth, cols), f32),
                field,
                field,
                field,
                field,
                pltpu.VMEM((2, depth, cols), f32),
                pltpu.VMEM((depth, cols), f32),
                pltpu.VMEM((4, 3 * rows, 2 * cols), f32),
                pltpu.VMEM((5, 3 * rows, 2 * cols), f32),
                pltpu.VMEM((8, 2 * cols), f32),
                dma((9,)),
                dma((8,)),
                dma((8,)),
                dma((6,)),
                dma((5,)),
                dma((1,)),
                dma((n_lon // GROUP,)),
                dma((n_lon // GROUP + 1,)),
                dma((n_lon // GROUP // 2 + 1,)),
                dma((GROUP,)),
                dma((GROUP,)),
                dma((2, GROUP)),
            ],
            compiler_params=pltpu.CompilerParams(collective_id=1, has_side_effects=True),
        )(
            tracer.reshape(depth * rows, cols),
            velocity.reshape(2 * depth * rows, cols),
            surface,
            transport.reshape(2 * rows, cols),
            levels,
            horiz_mixing,
            vert_mixing,
            land_tiles,
            fold_pair,
        )
        return (
            tracer_new.reshape(depth, rows, cols),
            surface_new,
            transport_new.reshape(2, rows, cols),
        )

    return jax.shard_map(
        shards,
        mesh=mesh,
        in_specs=(
            P("member", "lat", "lon"),
            P(None, "member", "lat", "lon"),
            P(("member", "lat"), "lon"),
            P("member", "lat", "lon"),
            P("member"),
            P("member"),
            P("lat", "lon"),
            P("lat", "lon"),
            P("lon"),
        ),
        out_specs=(
            P("member", "lat", "lon"),
            P(("member", "lat"), "lon"),
            P("member", "lat", "lon"),
        ),
        check_vma=False,
    )
```

```python
import functools

import jax
import jax.numpy as jnp
from jax import lax
from jax.experimental import pallas as pl
from jax.experimental.pallas import tpu as pltpu
from jax.sharding import PartitionSpec as P

SUB = 12
fb_step = 0.6
drag_rate = 0.02
MESH = pl.DeviceIdType.MESH

E, W, N, S, NE, NW, SE, SW = range(8)
OPPOSITE = {E: W, W: E, N: S, S: N, NE: SW, SW: NE, NW: SE, SE: NW}
STEP = {E: (0, 1), W: (0, -1), N: (1, 0), S: (-1, 0), NE: (1, 1), NW: (1, -1), SE: (-1, 1), SW: (-1, -1)}
GROUP = 4


def ocean_kernel(
    n_lon,
    n_lat,
    depth,
    rows,
    cols,
    tracer_hbm,
    velocity_hbm,
    surface_hbm,
    transport_hbm,
    levels_hbm,
    horiz_hbm,
    vert_hbm,
    land_hbm,
    fold_hbm,
    tracer_out,
    surface_out,
    transport_out,
    horiz,
    vert,
    land,
    fold,
    tr,
    vel,
    lev,
    own,
    halo,
    side_out,
    side_in,
    edge_lon,
    halo_lon,
    edge_lat,
    halo_lat,
    slab,
    hold,
    fwd_out,
    fwd_in,
    pick,
    fin,
    tfin,
    step_ref,
    cpl,
    rec,
    prime,
    face_lat,
    mix_rows,
    ext,
    coef,
    fold_fix,
    load_sem,
    halo_send,
    halo_recv,
    trac_send,
    trac_recv,
    hold_send,
    hold_recv,
    fwd_send,
    fwd_recv,
    fin_send,
    fin_recv,
    tfin_recv,
):
    lat = lax.axis_index("lat")
    lon = lax.axis_index("lon")
    top = lat == n_lat - 1
    bottom = lat == 0
    t_relay = n_lat - 3
    v_relay = 1
    is_t_relay = lat == t_relay
    is_v_relay = lat == v_relay
    relay = is_t_relay | is_v_relay
    ring = top | relay
    n_group = n_lon // GROUP
    me = lon & (GROUP - 1)
    group = lon - me
    keeper = lon < GROUP
    block = 4 * SUB + 8
    half_way = n_group // 2
    at_group = lon >> 2
    rising = at_group <= half_way
    blocks = jnp.where(rising, half_way + 2 - at_group, half_way + 1 - n_group + at_group)
    onward = jnp.where(rising, GROUP, -GROUP)
    has_next = jnp.logical_not(keeper) & (blocks > 2)
    has_previous = (at_group > 1) & (at_group < n_group - 1)

    def partner(g):
        return g * GROUP + (GROUP - 1 - me)

    def lon_at(step):
        return lax.rem(lon + step + n_lon, n_lon)

    def lat_at(step):
        return lax.rem(lat + step + n_lat, n_lat)

    def remote(src, dst, send, recv, to):
        return pltpu.make_async_remote_copy(
            src_ref=src, dst_ref=dst, send_sem=send, recv_sem=recv, device_id=to, device_id_type=MESH
        )

    small = [
        pltpu.make_async_copy(surface_hbm, own.at[pl.ds(0, rows)], load_sem.at[0]),
        pltpu.make_async_copy(transport_hbm, own.at[pl.ds(rows, 2 * rows)], load_sem.at[1]),
        pltpu.make_async_copy(levels_hbm, lev, load_sem.at[2]),
        pltpu.make_async_copy(land_hbm, land, load_sem.at[5]),
        pltpu.make_async_copy(fold_hbm, fold, load_sem.at[6]),
        pltpu.make_async_copy(horiz_hbm, horiz, load_sem.at[7]),
        pltpu.make_async_copy(vert_hbm, vert, load_sem.at[8]),
    ]
    large = [
        pltpu.make_async_copy(tracer_hbm, tr, load_sem.at[3]),
        pltpu.make_async_copy(velocity_hbm, vel, load_sem.at[4]),
    ]
    for copy in small:
        copy.start()
    barrier = pltpu.get_barrier_semaphore()
    peers = [STEP[side] for side in range(8)] + [(2, 0), (-2, 0)]
    for d_lat, d_lon in peers:
        pl.semaphore_signal(
            barrier, inc=1, device_id={"lat": lat_at(d_lat), "lon": lon_at(d_lon)}, device_id_type=MESH
        )

    @pl.when(ring)
    def _():
        @pl.when(keeper)
        def _():
            for g in range(1, n_group):
                pl.semaphore_signal(barrier, inc=1, device_id={"lon": partner(g)}, device_id_type=MESH)

        @pl.when(has_previous)
        def _():
            pl.semaphore_signal(barrier, inc=1, device_id={"lon": lon - onward}, device_id_type=MESH)

        for e in range(1, GROUP):
            pl.semaphore_signal(
                barrier, inc=1, device_id={"lon": group + ((me + e) & (GROUP - 1))}, device_id_type=MESH
            )

    for copy in large:
        copy.start()

    zeros_tile = jnp.zeros((4 * rows, cols), jnp.float32)

    @pl.when(bottom)
    def _():
        halo[1] = zeros_tile
        for side in (SE, SW):
            side_in[side] = jnp.zeros((8, cols), jnp.float32)
        halo_lat[1] = jnp.zeros((2 * depth, cols), jnp.float32)

    @pl.when(top)
    def _():
        halo[0] = zeros_tile
        for side in (NE, NW):
            side_in[side] = jnp.zeros((8, cols), jnp.float32)
        halo_lat[0] = jnp.zeros((2 * depth, cols), jnp.float32)

    for copy in small:
        copy.wait()
    dry = 1 - land[0, 0]
    own[pl.ds(3 * rows, rows), :] = (lev[...] * dry).astype(jnp.float32)

    lane8 = lax.broadcasted_iota(jnp.int32, (8, cols), 1)
    to_east, to_west = jnp.zeros((8, cols), jnp.float32), jnp.zeros((8, cols), jnp.float32)
    for k in range(8):
        here = (lane8 >> 4) == k
        part = own[pl.ds(8 * k, 8), :]
        to_east = jnp.where(here, pltpu.roll(part, (16 * k + 16) % cols, axis=1), to_east)
        to_west = jnp.where(here, pltpu.roll(part, 16 * k, axis=1) if k else part, to_west)
    side_out[0] = to_east
    side_out[1] = to_west

    @pl.when(top)
    def _():
        slab[pl.ds(block - 8, 8), :] = jnp.zeros((8, cols), jnp.float32)
        for f, (start, back, sign) in enumerate(((0, 0, 1), (rows, 0, -1), (3 * rows, 0, 1), (2 * rows, 1, -1))):
            for i in range(SUB):
                row = own[pl.ds(start + rows - 1 - i - back, 1), :]
                at = 8 * f + i if i < 8 else 32 + (SUB - 8) * f + i - 8
                slab[pl.ds(at, 1), :] = row if sign == 1 else -row
        slab[pl.ds(block - 8, 1), :] = -own[pl.ds(3 * rows - 1, 1), :]

    pl.semaphore_wait(barrier, len(peers) + jnp.where(ring, GROUP - jnp.where(keeper, 1, 0) + jnp.where(has_next, 1, 0), 0))

    pivot_col = lax.rem(fold[0] + lon * cols, n_lon * cols)
    q = lax.div(pivot_col, cols)
    r = lax.rem(pivot_col, cols)

    def halo_copy(side):
        d_lat, d_lon = STEP[side]
        slot = OPPOSITE[side]
        if d_lon == 0:
            src, dst = own, halo.at[0 if slot == N else 1]
        else:
            src, dst = side_out.at[0 if d_lon == 1 else 1], side_in.at[slot]
        return remote(
            src,
            dst,
            halo_send.at[side],
            halo_recv.at[slot],
            {"lat": lat_at(d_lat), "lon": lon_at(d_lon)},
        )

    def halo_wait(side):
        dst = halo.at[0 if side == N else 1] if side in (N, S) else side_in.at[side]
        remote(dst, dst, halo_send.at[side], halo_recv.at[side], {"lon": lon}).wait_recv()

    for side in (E, W):
        halo_copy(side).start()

    @pl.when(jnp.logical_not(top))
    def _():
        for side in (N, NE, NW):
            halo_copy(side).start()

    @pl.when(jnp.logical_not(bottom))
    def _():
        for side in (S, SE, SW):
            halo_copy(side).start()

    def hold_copy(size):
        slot = lon >> 2
        return remote(
            slab.at[pl.ds(0, size)],
            hold.at[slot, pl.ds(0, size)],
            hold_send.at[0],
            hold_recv.at[slot],
            {"lon": partner(0)},
        )

    def wanted(kind, to):
        low = q - to - 2 + 2 * n_lon
        return (low + ((kind - low) & (GROUP - 1))) & (n_lon - 1)

    def kind_of(place):
        return jnp.where(keeper, GROUP - 1 - place, place)

    def lowest(kind, g):
        return wanted(kind, g * GROUP + GROUP - 1) >> 2

    @pl.when(top)
    def _():
        hold_copy(block).start()

    for copy in large:
        copy.wait()
    u_base = 0
    v_base = depth * rows
    edge_lat[0, pl.ds(0, depth), :] = tr[pl.ds(rows - 1, depth, stride=rows), :]
    edge_lat[0, pl.ds(depth, depth), :] = vel[pl.ds(v_base + rows - 1, depth, stride=rows), :]
    edge_lat[1, pl.ds(0, depth), :] = tr[pl.ds(0, depth, stride=rows), :]
    edge_lat[1, pl.ds(depth, depth), :] = vel[pl.ds(v_base, depth, stride=rows), :]

    def spread_copy(j):
        to = (t_relay, v_relay)[j]
        return remote(
            edge_lat.at[0, pl.ds(j * depth, depth)],
            slab.at[pl.ds(0, depth)],
            trac_send.at[j],
            trac_recv.at[4],
            {"lat": to},
        )

    def lat_copy(north):
        slot = 1 if north else 0
        return remote(
            edge_lat.at[0 if north else 1],
            halo_lat.at[slot],
            trac_send.at[0 if north else 2],
            trac_recv.at[slot],
            {"lat": lat_at(1 if north else -1)},
        )

    @pl.when(top)
    def _():
        spread_copy(0).start()
        spread_copy(1).start()

    @pl.when(jnp.logical_not(top))
    def _():
        lat_copy(True).start()

    @pl.when(jnp.logical_not(bottom))
    def _():
        lat_copy(False).start()

    half = lane8 >> 1

    def pack(l, carry):
        pt, pu = carry
        for g in range(2):
            item = l + depth * g
            here = half == jnp.full((8, cols), item, jnp.int32)
            at = pl.multiple_of(l * rows + 8 * g, 8)
            pt = jnp.where(here, pltpu.roll(tr[pl.ds(at, 8), :], 2 * item + 1, axis=1), pt)
            pu = jnp.where(here, pltpu.roll(vel[pl.ds(at, 8), :], 2 * item + 1, axis=1), pu)
        return pt, pu

    pt, pu = lax.fori_loop(
        0, depth, pack, (jnp.zeros((8, cols), jnp.float32), jnp.zeros((8, cols), jnp.float32)), unroll=4
    )
    edge_lon[pl.ds(0, 8), :] = pt
    edge_lon[pl.ds(8, 8), :] = pu

    def lon_copy(east):
        slot = 1 if east else 0
        return remote(
            edge_lon,
            halo_lon.at[slot],
            trac_send.at[3 if east else 4],
            trac_recv.at[2 + slot],
            {"lon": lon_at(1 if east else -1)},
        )

    lon_copy(True).start()
    lon_copy(False).start()


    def trac_wait(dst, sem):
        remote(dst, dst, trac_send.at[5], sem, {"lon": lon}).wait_recv()

    @pl.when(relay)
    def _():
        trac_wait(slab.at[pl.ds(0, depth)], trac_recv.at[4])
        hold_copy(depth).start()

    h_own = own[pl.ds(3 * rows, rows), :]

    def pivots(l, carry):
        c_up, p_up = carry
        wet_below = (jnp.full((rows, cols), (l + 1).astype(jnp.float32)) < h_own).astype(jnp.float32)
        c_down = vert[jnp.minimum(l, depth - 2)] * wet_below
        pivot = (1.0 + c_up + c_down) + c_up * p_up
        inv = 1.0 / pivot
        p_down = -c_down * inv
        at = pl.ds(pl.multiple_of(l * rows, rows), rows)
        cpl[at, :] = c_up
        rec[at, :] = inv
        prime[at, :] = p_down
        mix_rows[pl.ds(l, 1), :] = jnp.full((1, cols), horiz[l])
        return c_down, p_down

    zero = jnp.zeros((rows, cols), jnp.float32)
    lax.fori_loop(0, depth, pivots, (zero, zero), unroll=2)

    lane16 = lax.broadcasted_iota(jnp.int32, (rows, cols), 1)
    row16 = lax.broadcasted_iota(jnp.int32, (rows, cols), 0)
    last_col = lane16 == cols - 1
    first_col = lane16 == 0
    last_row = row16 == rows - 1
    first_row = row16 == 0
    h_e = jnp.where(last_col, 0.0, pltpu.roll(h_own, cols - 1, axis=1))
    h_n = jnp.where(last_row, 0.0, pltpu.roll(h_own, rows - 1, axis=0))

    def fluxes(l, carry):
        at = pl.ds(pl.multiple_of(l * rows, rows), rows)
        t = tr[at, :]
        u = vel[at, :]
        v = vel[pl.ds(pl.multiple_of(v_base + l * rows, rows), rows), :]
        m = horiz[l]
        level = jnp.full((rows, cols), l.astype(jnp.float32))
        wet = (level < h_own).astype(jnp.float32)
        wet_e = (level < h_e).astype(jnp.float32)
        wet_n = (level < h_n).astype(jnp.float32)
        t_e = pltpu.roll(t, cols - 1, axis=1)
        u_e = pltpu.roll(u, cols - 1, axis=1)
        f_e = wet * wet_e * (m * (t_e - t) - 0.25 * (u + u_e) * (t + t_e))
        f_w = pltpu.roll(f_e, 1, axis=1)
        t_n = pltpu.roll(t, rows - 1, axis=0)
        v_n = pltpu.roll(v, rows - 1, axis=0)
        f_n = wet * wet_n * (m * (t_n - t) - 0.25 * (v + v_n) * (t + t_n))
        f_s = pltpu.roll(f_n, 1, axis=0)
        step_ref[at, :] = wet * (t + ((f_e - f_w) + (f_n - f_s)))
        return carry

    lax.fori_loop(0, depth, fluxes, 0, unroll=4)

    def final_copy(e, size, dst, recv):
        return remote(
            pick.at[e, pl.ds(0, size)], dst, fin_send.at[e], recv, {"lat": n_lat - 1, "lon": group + e}
        )

    def forward_copy(out, slot, to, size):
        return remote(
            fwd_out.at[out, pl.ds(0, size)], fwd_in.at[slot, pl.ds(0, size)], fwd_send.at[out], fwd_recv.at[slot], {"lon": to}
        )

    def chain_copy(slot, size):
        return remote(
            fwd_in.at[slot, pl.ds(0, size)],
            fwd_in.at[slot - 1, pl.ds(0, size)],
            fwd_send.at[slot],
            fwd_recv.at[slot - 1],
            {"lon": lon + onward},
        )

    def chain_wait(slot, size):
        dst = fwd_in.at[slot, pl.ds(0, size)]
        remote(dst, dst, fwd_send.at[0], fwd_recv.at[slot], {"lon": partner(0)}).wait_recv()

    rise, fall = half_way + 1, half_way

    def serve(size, block, target):
        def send(e, carry):
            pick[e, pl.ds(0, size), :] = block(e)
            target(e)
            return carry

        lax.fori_loop(0, GROUP, send, 0)

    def to_top(e):
        @pl.when(e != me)
        def _():
            final_copy(e, block, fin.at[me], fin_recv.at[me]).start()

    def to_relayed(j):
        return lambda e: final_copy(e, depth, tfin.at[j, me], tfin_recv.at[j, me]).start()

    members = ((top, block, to_top), (is_t_relay, depth, to_relayed(0)), (is_v_relay, depth, to_relayed(1)))

    for role, size, target in members:

        @pl.when(role & keeper)
        def _(size=size, target=target):
            for g in range(n_group):
                dst = hold.at[g, pl.ds(0, size)]
                remote(dst, dst, hold_send.at[0], hold_recv.at[g], {"lon": partner(0)}).wait_recv()
            serve(size, lambda e: hold[wanted(GROUP - 1 - me, e) >> 2, pl.ds(0, size), :], target)

            first_up = lowest(GROUP - 1 - me, 1)
            first_down = lowest(GROUP - 1 - me, n_group - 1)

            def forward_up(j, carry):
                slot = (first_up + 1 - j + n_group) & (n_group - 1)
                fwd_out[j, pl.ds(0, size), :] = hold[slot, pl.ds(0, size), :]
                forward_copy(j, j, partner(1), size).start()
                return carry

            def forward_down(j, carry):
                slot = (first_down + j) & (n_group - 1)
                fwd_out[rise + j, pl.ds(0, size), :] = hold[slot, pl.ds(0, size), :]
                forward_copy(rise + j, j, partner(n_group - 1), size).start()
                return carry

            lax.fori_loop(0, rise, forward_up, 0)
            lax.fori_loop(0, fall, forward_down, 0)

    for side in (E, W):
        halo_wait(side)

    @pl.when(jnp.logical_not(top))
    def _():
        for side in (N, NE, NW):
            halo_wait(side)

    @pl.when(jnp.logical_not(bottom))
    def _():
        for side in (S, SE, SW):
            halo_wait(side)

    near = lane8 < cols // 2
    west_half, east_half = pl.ds(0, cols), pl.ds(cols, cols)

    low, high = SUB, SUB + rows

    def beside(east, west, base, first, last):
        for k in range(8):
            tile = jnp.where(
                near,
                pltpu.roll(side_in[east], (cols - 16 * k) % cols, axis=1),
                pltpu.roll(side_in[west], (cols - 16 - 16 * k) % cols, axis=1),
            )
            at = 8 * (k % 2)
            lo, hi = max(first, at), min(last, at + 8)
            ext[k // 2, pl.ds(base + lo - first, hi - lo), east_half] = tile[lo - at : hi - at]

    beside(SE, SW, 0, rows - SUB, rows)
    beside(E, W, low, 0, rows)
    for f in range(4):
        ext[f, pl.ds(0, SUB), west_half] = halo[1, pl.ds((f + 1) * rows - SUB, SUB), :]
        ext[f, pl.ds(low, rows), west_half] = own[pl.ds(f * rows, rows), :]
    fold_fix[...] = jnp.zeros((8, 2 * cols), jnp.float32)

    @pl.when(jnp.logical_not(top))
    def _():
        beside(NE, NW, high, 0, SUB)
        for f in range(4):
            ext[f, pl.ds(high, SUB), west_half] = halo[0, pl.ds(f * rows, SUB), :]

    trac_wait(halo_lon.at[0], trac_recv.at[2])
    trac_wait(halo_lon.at[1], trac_recv.at[3])

    @pl.when(jnp.logical_not(top))
    def _():
        trac_wait(halo_lat.at[0], trac_recv.at[0])

    @pl.when(jnp.logical_not(bottom))
    def _():
        trac_wait(halo_lat.at[1], trac_recv.at[1])

    even = (lane8 & 1) == 0
    h_beside = ext[3, pl.ds(low, rows), east_half]
    h_north_row = halo[0, pl.ds(3 * rows, 1), :]
    h_south_row = halo[1, pl.ds(4 * rows - 1, 1), :]

    def swap(from_east, from_west):
        return jnp.where(
            even, pltpu.roll(from_east, cols - 1, axis=1), pltpu.roll(from_west, 1, axis=1)
        )

    pt = edge_lon[pl.ds(0, 8), :]
    pu = edge_lon[pl.ds(8, 8), :]
    th = swap(halo_lon[0, pl.ds(0, 8), :], halo_lon[1, pl.ds(0, 8), :])
    uh = swap(halo_lon[0, pl.ds(8, 8), :], halo_lon[1, pl.ds(8, 8), :])

    def column(tile, at):
        lo = jnp.broadcast_to(tile[0:8, at : at + 1], (8, cols))
        hi = jnp.broadcast_to(tile[8:16, at : at + 1], (8, cols))
        return jnp.where(half < depth, lo, hi)

    level_of = (half & (depth - 1)).astype(jnp.float32)
    h_in = jnp.where(even, column(h_own, cols - 1), column(h_own, 0))
    h_out = jnp.where(even, column(h_beside, 0), column(h_beside, cols - 1))
    wet_pair = (level_of < h_in).astype(jnp.float32) * (level_of < h_out).astype(jnp.float32)

    def lane_mix(l, acc):
        return jnp.where((half & (depth - 1)) == jnp.full((8, cols), l, jnp.int32), horiz[l], acc)

    mix_lanes = lax.fori_loop(0, depth, lane_mix, jnp.zeros((8, cols), jnp.float32), unroll=4)
    sign = jnp.where(even, 1.0, -1.0)
    side_flux = wet_pair * (mix_lanes * (th - pt) - sign * (0.25 * (pu + uh) * (pt + th)))

    level_row = lax.broadcasted_iota(jnp.int32, (depth, cols), 0).astype(jnp.float32)

    def row_face(low_t, low_v, high_t, high_v, h_low, h_high):
        wet = (level_row < h_low).astype(jnp.float32) * (level_row < h_high).astype(jnp.float32)
        return wet * (mix_rows[...] * (high_t - low_t) - 0.25 * (low_v + high_v) * (low_t + high_t))

    first, second = pl.ds(0, depth), pl.ds(depth, depth)
    face_lat[0] = row_face(
        edge_lat[0, first, :], edge_lat[0, second, :], halo_lat[0, first, :], halo_lat[0, second, :],
        own[pl.ds(4 * rows - 1, 1), :], h_north_row,
    )
    face_lat[1] = row_face(
        halo_lat[1, first, :], halo_lat[1, second, :], edge_lat[1, first, :], edge_lat[1, second, :],
        h_south_row, own[pl.ds(3 * rows, 1), :],
    )

    rim_col = last_col | first_col

    def forward(l, sweep):
        at = pl.ds(pl.multiple_of(l * rows, rows), rows)
        rim = jnp.concatenate(
            [
                pltpu.roll(side_flux, cols - 1 - 2 * l, axis=1),
                pltpu.roll(side_flux, lax.rem(2 * cols - 1 - 2 * (l + depth), cols), axis=1),
            ],
            axis=0,
        )
        gain = jnp.where(rim_col, rim, 0.0) + (
            jnp.where(last_row, face_lat[0, pl.ds(l, 1), :], 0.0)
            - jnp.where(first_row, face_lat[1, pl.ds(l, 1), :], 0.0)
        )
        sweep = ((step_ref[at, :] + gain) + cpl[at, :] * sweep) * rec[at, :]
        step_ref[at, :] = sweep
        return sweep

    lax.fori_loop(0, depth, forward, zero, unroll=4)

    def backward(i, x):
        l = depth - 1 - i
        at = pl.ds(pl.multiple_of(l * rows, rows), rows)
        x = step_ref[at, :] - prime[at, :] * x
        tracer_out[at, :] = x
        return x

    lax.fori_loop(0, depth, backward, zero, unroll=4)

    for role, size, target in members:

        @pl.when(role & jnp.logical_not(keeper))
        def _(size=size, target=target):
            chain_wait(0, size)
            chain_wait(1, size)

            @pl.when(has_next)
            def _():
                chain_copy(1, size).start()

            first_slot = lowest(me, at_group)
            turned = jnp.where(rising, 1, 0)

            def either(e):
                which = ((wanted(me, group + e) >> 2) - first_slot + turned) & 1
                return jnp.where(
                    jnp.full((size, cols), which, jnp.int32) == 1,
                    fwd_in[1, pl.ds(0, size), :],
                    fwd_in[0, pl.ds(0, size), :],
                )

            serve(size, either, target)

            def hand_on(slot, carry):
                chain_wait(slot, size)
                chain_copy(slot, size).start()
                return carry

            lax.fori_loop(2, blocks, hand_on, 0)

    def source_of(shape, shift, isu):
        s = lax.broadcasted_iota(jnp.int32, shape, 1)
        l = (jnp.full(shape, r, jnp.int32) - isu - s) & (cols - 1)
        return s, l

    @pl.when(top)
    def _():
        shape = (block, cols)
        row = lax.broadcasted_iota(jnp.int32, shape, 0)
        isu = (((row >= 8) & (row < 16)) | ((row >= 24 + SUB) & (row < 16 + 2 * SUB))).astype(jnp.int32)
        s, l = source_of(shape, 0, isu)
        whole = n_lon * cols
        base = jnp.full(shape, pivot_col - lon * cols + 2 * whole, jnp.int32) - isu
        dev_main = ((base - l) & (whole - 1)) >> 7
        off = jnp.where(l < cols // 2, cols, -cols)
        dev_side = ((base - l - off) & (whole - 1)) >> 7
        main = jnp.zeros(shape, jnp.float32)
        side = main
        for e in range(GROUP):
            @pl.when(e != me)
            def _():
                trac_wait(fin.at[e], fin_recv.at[e])

            @pl.when(e == me)
            def _():
                fin[e] = pick[e]

        for e in range(GROUP):
            got = fin[e]
            src = jnp.full(shape, wanted(kind_of(e), lon), jnp.int32)
            main = jnp.where(dev_main == src, got, main)
            side = jnp.where(dev_side == src, got, side)
        main = jnp.take_along_axis(main, l, axis=1)
        side = jnp.take_along_axis(side, l, axis=1)
        for f in range(4):
            ff = (0, 1, 3, 2)[f]
            rest = 32 + (SUB - 8) * f
            for half_of, part in ((west_half, main), (east_half, side)):
                ext[ff, pl.ds(high, 8), half_of] = part[8 * f : 8 * f + 8]
                ext[ff, pl.ds(high + 8, SUB - 8), half_of] = part[rest : rest + SUB - 8]
        for half_of, part in ((west_half, main), (east_half, side)):
            fold_fix[pl.ds(high - 24, 1), half_of] = part[block - 8 : block - 7] - ext[2, pl.ds(high - 1, 1), half_of]

    wide = 2 * cols
    tall = rows + 2 * SUB
    h = ext[3]
    sea = (h > 0.0).astype(jnp.float32)

    def east(x):
        return pltpu.roll(x, wide - 1, axis=1)

    def north(x):
        return pltpu.roll(x, tall - 1, axis=0)

    zonal_mask = sea * east(sea)
    merid_mask = sea * north(sea)
    coef[0] = fb_step * ((h + east(h)) / (2.0 * depth)) * zonal_mask
    coef[1] = (1.0 - drag_rate) * zonal_mask
    coef[2] = fb_step * ((h + north(h)) / (2.0 * depth)) * merid_mask
    coef[3] = (1.0 - drag_rate) * merid_mask
    coef[4] = fb_step * sea
    fix_decay = pltpu.roll(coef[3], 1, axis=0)[24:32]

    def cycle(i, state):
        eta, u, v, fix = state
        v_south = pltpu.roll(v, 1, axis=0)
        v_south = jnp.concatenate(
            [v_south[:24], v_south[24:32] + fix, v_south[32:]], axis=0
        )
        div = (u - pltpu.roll(u, 1, axis=1)) + (v - v_south)
        eta = eta - coef[4] * div
        u = u * coef[1] - coef[0] * (east(eta) - eta)
        v = v * coef[3] - coef[2] * (north(eta) - eta)
        return eta, u, v, fix * fix_decay

    eta, u, v, _ = lax.fori_loop(0, SUB, cycle, (ext[0] * sea, ext[1], ext[2], fold_fix[...]))
    surface_out[...] = eta[low:high, :cols]
    transport_out[pl.ds(0, rows), :] = u[low:high, :cols]
    transport_out[pl.ds(rows, rows), :] = v[low:high, :cols]

    @pl.when(top)
    def _():
        got = []
        for j in range(2):
            shape = (depth, cols)
            s, l = source_of(shape, 0, 0)
            whole = n_lon * cols
            dev = ((jnp.full(shape, pivot_col - lon * cols + 2 * whole, jnp.int32) - l) & (whole - 1)) >> 7
            acc = jnp.zeros(shape, jnp.float32)
            for e in range(GROUP):
                trac_wait(tfin.at[j, e], tfin_recv.at[j, e])
                acc = jnp.where(dev == jnp.full(shape, wanted(kind_of(e), lon), jnp.int32), tfin[j, e], acc)
            got.append(jnp.take_along_axis(acc, l, axis=1))
        h_last = own[pl.ds(4 * rows - 1, 1), :]
        flux = row_face(
            edge_lat[0, first, :], edge_lat[0, second, :], got[0], got[1], h_last, ext[3, pl.ds(high, 1), west_half]
        )
        face_lat[0] = (level_row < h_last).astype(jnp.float32) * flux
        c_last = cpl[pl.ds(rows - 1, depth, stride=rows), :]
        r_last = rec[pl.ds(rows - 1, depth, stride=rows), :]
        p_last = prime[pl.ds(rows - 1, depth, stride=rows), :]
        out_last = tracer_out[pl.ds(rows - 1, depth, stride=rows), :]
        delta = face_lat[0]
        sweeps = []
        x = jnp.zeros((1, cols), jnp.float32)
        for k in range(depth):
            x = (delta[k : k + 1] + c_last[k : k + 1] * x) * r_last[k : k + 1]
            sweeps.append(x)
        x = jnp.zeros((1, cols), jnp.float32)
        for k in range(depth - 1, -1, -1):
            x = sweeps[k] - p_last[k : k + 1] * x
            tracer_out[pl.ds(k * rows + rows - 1, 1), :] = out_last[k : k + 1] + x

    for side in (E, W):
        halo_copy(side).wait_send()
    lon_copy(True).wait_send()
    lon_copy(False).wait_send()

    @pl.when(jnp.logical_not(top))
    def _():
        for side in (N, NE, NW):
            halo_copy(side).wait_send()
        lat_copy(True).wait_send()

    @pl.when(jnp.logical_not(bottom))
    def _():
        for side in (S, SE, SW):
            halo_copy(side).wait_send()
        lat_copy(False).wait_send()

    @pl.when(top)
    def _():
        spread_copy(0).wait_send()
        spread_copy(1).wait_send()

        hold_copy(block).wait_send()

        @pl.when(keeper)
        def _():
            for j in range(rise):
                forward_copy(j, j, partner(1), block).wait_send()
            for j in range(fall):
                forward_copy(rise + j, j, partner(n_group - 1), block).wait_send()

        @pl.when(has_next)
        def _():
            def gone(slot, carry):
                chain_copy(slot, block).wait_send()
                return carry

            lax.fori_loop(1, blocks, gone, 0)

        for e in range(GROUP):

            @pl.when(e != me)
            def _(e=e):
                final_copy(e, block, fin.at[me], fin_recv.at[me]).wait_send()

    @pl.when(relay)
    def _():
        hold_copy(depth).wait_send()

        @pl.when(keeper)
        def _():
            for j in range(rise):
                forward_copy(j, j, partner(1), depth).wait_send()
            for j in range(fall):
                forward_copy(rise + j, j, partner(n_group - 1), depth).wait_send()

        @pl.when(has_next)
        def _():
            def gone(slot, carry):
                chain_copy(slot, depth).wait_send()
                return carry

            lax.fori_loop(1, blocks, gone, 0)

        for e in range(GROUP):
            final_copy(e, depth, tfin.at[0, me], tfin_recv.at[0, me]).wait_send()


def write_out(a, b, c, a_hbm, b_hbm, c_hbm, sem):
    copies = [
        pltpu.make_async_copy(src, dst, sem.at[i])
        for i, (src, dst) in enumerate(((a, a_hbm), (b, b_hbm), (c, c_hbm)))
    ]
    for copy in copies:
        copy.start()
    for copy in copies:
        copy.wait()


def solution(mesh):
    n_lon, n_lat = mesh.shape["lon"], mesh.shape["lat"]

    def shards(tracer, velocity, surface, transport, horiz_mixing, vert_mixing, levels, land_tiles, fold_pair):
        depth, rows, cols = tracer.shape
        f32 = jnp.float32
        hbm = pl.BlockSpec(memory_space=pl.ANY)
        vmem = pl.BlockSpec(memory_space=pltpu.VMEM)
        dma = pltpu.SemaphoreType.DMA
        field = pltpu.VMEM((depth * rows, cols), f32)
        results = pl.pallas_call(
            functools.partial(ocean_kernel, n_lon, n_lat, depth, rows, cols),
            name="ocean",
            out_shape=(
                pltpu.VMEM((depth * rows, cols), f32),
                pltpu.VMEM((rows, cols), f32),
                pltpu.VMEM((2 * rows, cols), f32),
            ),
            in_specs=[hbm] * 9,
            out_specs=(vmem, vmem, vmem),
            scratch_shapes=[
                pltpu.SMEM((depth,), f32),
                pltpu.SMEM((depth - 1,), f32),
                pltpu.SMEM((1, 1), jnp.int32),
                pltpu.SMEM((cols,), jnp.int32),
                field,
                pltpu.VMEM((2 * depth * rows, cols), f32),
                pltpu.VMEM((rows, cols), jnp.int32),
                pltpu.VMEM((4 * rows, cols), f32),
                pltpu.VMEM((2, 4 * rows, cols), f32),
                pltpu.VMEM((2, 8, cols), f32),
                pltpu.VMEM((8, 8, cols), f32),
                pltpu.VMEM((16, cols), f32),
                pltpu.VMEM((2, 16, cols), f32),
                pltpu.VMEM((2, 2 * depth, cols), f32),
                pltpu.VMEM((2, 2 * depth, cols), f32),
                pltpu.VMEM((4 * SUB + 8, cols), f32),
                pltpu.VMEM((n_lon // GROUP, 4 * SUB + 8, cols), f32),
                pltpu.VMEM((n_lon // GROUP + 1, 4 * SUB + 8, cols), f32),
                pltpu.VMEM((n_lon // GROUP // 2 + 1, 4 * SUB + 8, cols), f32),
                pltpu.VMEM((GROUP, 4 * SUB + 8, cols), f32),
                pltpu.VMEM((GROUP, 4 * SUB + 8, cols), f32),
                pltpu.VMEM((2, GROUP, depth, cols), f32),
                field,
                field,
                field,
                field,
                pltpu.VMEM((2, depth, cols), f32),
                pltpu.VMEM((depth, cols), f32),
                pltpu.VMEM((4, rows + 2 * SUB, 2 * cols), f32),
                pltpu.VMEM((5, rows + 2 * SUB, 2 * cols), f32),
                pltpu.VMEM((8, 2 * cols), f32),
                dma((9,)),
                dma((8,)),
                dma((8,)),
                dma((6,)),
                dma((5,)),
                dma((1,)),
                dma((n_lon // GROUP,)),
                dma((n_lon // GROUP + 1,)),
                dma((n_lon // GROUP // 2 + 1,)),
                dma((GROUP,)),
                dma((GROUP,)),
                dma((2, GROUP)),
            ],
            compiler_params=pltpu.CompilerParams(collective_id=1, has_side_effects=True),
        )(
            tracer.reshape(depth * rows, cols),
            velocity.reshape(2 * depth * rows, cols),
            surface,
            transport.reshape(2 * rows, cols),
            levels,
            horiz_mixing,
            vert_mixing,
            land_tiles,
            fold_pair,
        )
        results = [pltpu.with_memory_space_constraint(result, pltpu.VMEM) for result in results]
        tracer_new, surface_new, transport_new = pl.pallas_call(
            write_out,
            name="write_out",
            out_shape=tuple(jax.ShapeDtypeStruct(result.shape, f32) for result in results),
            in_specs=[vmem] * 3,
            out_specs=(hbm,) * 3,
            scratch_shapes=[dma((3,))],
        )(*results)
        return (
            tracer_new.reshape(depth, rows, cols),
            surface_new,
            transport_new.reshape(2, rows, cols),
        )

    return jax.shard_map(
        shards,
        mesh=mesh,
        in_specs=(
            P("member", "lat", "lon"),
            P(None, "member", "lat", "lon"),
            P(("member", "lat"), "lon"),
            P("member", "lat", "lon"),
            P("member"),
            P("member"),
            P("lat", "lon"),
            P("lat", "lon"),
            P("lon"),
        ),
        out_specs=(
            P("member", "lat", "lon"),
            P(("member", "lat"), "lon"),
            P("member", "lat", "lon"),
        ),
        check_vma=False,
    )
```

```python
import functools

import jax
import jax.numpy as jnp
from jax import lax
from jax.experimental import pallas as pl
from jax.experimental.pallas import tpu as pltpu
from jax.sharding import PartitionSpec as P

SUB = 12
fb_step = 0.6
drag_rate = 0.02
MESH = pl.DeviceIdType.MESH

E, W, N, S, NE, NW, SE, SW = range(8)
OPPOSITE = {E: W, W: E, N: S, S: N, NE: SW, SW: NE, NW: SE, SE: NW}
STEP = {E: (0, 1), W: (0, -1), N: (1, 0), S: (-1, 0), NE: (1, 1), NW: (1, -1), SE: (-1, 1), SW: (-1, -1)}
GROUP = 4


def ocean_kernel(
    n_lon,
    n_lat,
    depth,
    rows,
    cols,
    tracer_hbm,
    velocity_hbm,
    surface_hbm,
    transport_hbm,
    levels_hbm,
    horiz_hbm,
    vert_hbm,
    land_hbm,
    fold_hbm,
    tracer_out,
    surface_out,
    transport_out,
    horiz,
    vert,
    land,
    fold,
    tr,
    vel,
    lev,
    own,
    halo,
    side_out,
    side_in,
    edge_lon,
    halo_lon,
    edge_lat,
    halo_lat,
    slab,
    hold,
    fwd_out,
    fwd_in,
    pick,
    fin,
    tfin,
    step_ref,
    cpl,
    rec,
    prime,
    face_lat,
    mix_rows,
    ext,
    coef,
    fold_fix,
    load_sem,
    hello,
    halo_send,
    halo_recv,
    trac_send,
    trac_recv,
    hold_send,
    hold_recv,
    fwd_send,
    fwd_recv,
    fin_send,
    fin_recv,
    tfin_recv,
):
    lat = lax.axis_index("lat")
    lon = lax.axis_index("lon")
    top = lat == n_lat - 1
    bottom = lat == 0
    t_relay = n_lat - 3
    v_relay = 1
    is_t_relay = lat == t_relay
    is_v_relay = lat == v_relay
    relay = is_t_relay | is_v_relay
    ring = top | relay
    n_group = n_lon // GROUP
    me = lon & (GROUP - 1)
    group = lon - me
    keeper = lon < GROUP
    block = 4 * SUB + 8
    half_way = n_group // 2
    at_group = lon >> 2
    rising = at_group <= half_way
    blocks = jnp.where(rising, half_way + 2 - at_group, half_way + 1 - n_group + at_group)
    onward = jnp.where(rising, GROUP, -GROUP)
    has_next = jnp.logical_not(keeper) & (blocks > 2)
    has_previous = (at_group > 1) & (at_group < n_group - 1)

    def partner(g):
        return g * GROUP + (GROUP - 1 - me)

    def lon_at(step):
        return lax.rem(lon + step + n_lon, n_lon)

    def lat_at(step):
        return lax.rem(lat + step + n_lat, n_lat)

    def remote(src, dst, send, recv, to):
        return pltpu.make_async_remote_copy(
            src_ref=src, dst_ref=dst, send_sem=send, recv_sem=recv, device_id=to, device_id_type=MESH
        )

    small = [
        pltpu.make_async_copy(surface_hbm, own.at[pl.ds(0, rows)], load_sem.at[0]),
        pltpu.make_async_copy(transport_hbm, own.at[pl.ds(rows, 2 * rows)], load_sem.at[1]),
        pltpu.make_async_copy(levels_hbm, lev, load_sem.at[2]),
        pltpu.make_async_copy(land_hbm, land, load_sem.at[5]),
        pltpu.make_async_copy(fold_hbm, fold, load_sem.at[6]),
        pltpu.make_async_copy(horiz_hbm, horiz, load_sem.at[7]),
        pltpu.make_async_copy(vert_hbm, vert, load_sem.at[8]),
    ]
    large = [
        pltpu.make_async_copy(tracer_hbm, tr, load_sem.at[3]),
        pltpu.make_async_copy(velocity_hbm, vel, load_sem.at[4]),
    ]
    for copy in small:
        copy.start()
    barrier = pltpu.get_barrier_semaphore()

    def signal(sem, d_lat, to):
        pl.semaphore_signal(
            sem, inc=1, device_id={"lat": lat_at(d_lat), "lon": to}, device_id_type=MESH
        )

    first_lon, last_lon = lon == 0, lon == n_lon - 1

    def signal_side(sem, d_lon):
        for d_lat in (-1, 0, 1):
            signal(sem, d_lat, lon_at(d_lon))

    for d_lat in (-2, -1, 1, 2):
        signal(barrier, d_lat, lon)

    @pl.when(jnp.logical_not(last_lon))
    def _():
        signal_side(barrier, 1)

    @pl.when(first_lon)
    def _():
        signal_side(barrier, -1)

    @pl.when(ring)
    def _():
        @pl.when(keeper)
        def _():
            for g in range(1, n_group):
                signal(barrier, 0, partner(g))

        @pl.when(has_previous & jnp.logical_not(rising))
        def _():
            signal(barrier, 0, lon - onward)

        @pl.when(has_next & rising)
        def _():
            signal(barrier, 0, lon + onward)

        for place in range(1, GROUP):

            @pl.when(place > me)
            def _(place=place):
                signal(barrier, 0, group + place)

    for copy in large:
        copy.start()

    zeros_tile = jnp.zeros((4 * rows, cols), jnp.float32)

    @pl.when(bottom)
    def _():
        halo[1] = zeros_tile
        for side in (SE, SW):
            side_in[side] = jnp.zeros((8, cols), jnp.float32)
        halo_lat[1] = jnp.zeros((2 * depth, cols), jnp.float32)

    @pl.when(top)
    def _():
        halo[0] = zeros_tile
        for side in (NE, NW):
            side_in[side] = jnp.zeros((8, cols), jnp.float32)
        halo_lat[0] = jnp.zeros((2 * depth, cols), jnp.float32)

    for copy in small[:4]:
        copy.wait()
    dry = 1 - land[0, 0]
    own[pl.ds(3 * rows, rows), :] = (lev[...] * dry).astype(jnp.float32)

    lane8 = lax.broadcasted_iota(jnp.int32, (8, cols), 1)
    to_east, to_west = jnp.zeros((8, cols), jnp.float32), jnp.zeros((8, cols), jnp.float32)
    for k in range(8):
        here = (lane8 >> 4) == k
        part = own[pl.ds(8 * k, 8), :]
        to_east = jnp.where(here, pltpu.roll(part, (16 * k + 16) % cols, axis=1), to_east)
        to_west = jnp.where(here, pltpu.roll(part, 16 * k, axis=1) if k else part, to_west)
    side_out[0] = to_east
    side_out[1] = to_west

    @pl.when(top)
    def _():
        slab[pl.ds(block - 8, 8), :] = jnp.zeros((8, cols), jnp.float32)
        for f, (start, back, sign) in enumerate(((0, 0, 1), (rows, 0, -1), (3 * rows, 0, 1), (2 * rows, 1, -1))):
            for i in range(SUB):
                row = own[pl.ds(start + rows - 1 - i - back, 1), :]
                at = 8 * f + i if i < 8 else 32 + (SUB - 8) * f + i - 8
                slab[pl.ds(at, 1), :] = row if sign == 1 else -row
        slab[pl.ds(block - 8, 1), :] = -own[pl.ds(3 * rows - 1, 1), :]

    def count(flag, n=1):
        return jnp.where(flag, n, 0)

    chained = (rising & has_previous) | (jnp.logical_not(rising) & has_next)
    lower_ring = me + count(jnp.logical_not(keeper)) + count(chained)
    pl.semaphore_wait(barrier, 4 + count(jnp.logical_not(first_lon), 3) + count(last_lon, 3) + count(ring, lower_ring))

    @pl.when(jnp.logical_not(first_lon))
    def _():
        signal_side(hello.at[0], -1)

    @pl.when(last_lon)
    def _():
        signal_side(hello.at[0], 1)

    @pl.when(ring)
    def _():
        for place in range(GROUP - 1):

            @pl.when(place < me)
            def _(place=place):
                signal(hello.at[1], 0, group + place)

        @pl.when(has_previous & rising)
        def _():
            signal(hello.at[1], 0, lon - onward)

    def ring_hello():
        later = GROUP - 1 - me + count(has_next & rising)

        @pl.when(later > 0)
        def _():
            pl.semaphore_wait(hello.at[1], later)

    @pl.when(ring & keeper)
    def _():
        ring_hello()

    def hold_copy(size):
        slot = lon >> 2
        return remote(
            slab.at[pl.ds(0, size)],
            hold.at[slot, pl.ds(0, size)],
            hold_send.at[0],
            hold_recv.at[slot],
            {"lon": partner(0)},
        )

    @pl.when(top)
    def _():
        hold_copy(block).start()

    for copy in small[4:]:
        copy.wait()
    pivot_col = lax.rem(fold[0] + lon * cols, n_lon * cols)
    q = lax.div(pivot_col, cols)
    r = lax.rem(pivot_col, cols)

    def halo_copy(side):
        d_lat, d_lon = STEP[side]
        slot = OPPOSITE[side]
        if d_lon == 0:
            src, dst = own, halo.at[0 if slot == N else 1]
        else:
            src, dst = side_out.at[0 if d_lon == 1 else 1], side_in.at[slot]
        return remote(
            src,
            dst,
            halo_send.at[side],
            halo_recv.at[slot],
            {"lat": lat_at(d_lat), "lon": lon_at(d_lon)},
        )

    def halo_wait(side):
        dst = halo.at[0 if side == N else 1] if side in (N, S) else side_in.at[side]
        remote(dst, dst, halo_send.at[side], halo_recv.at[side], {"lon": lon}).wait_recv()

    def halo_side(d_lon, act):
        act(halo_copy(E if d_lon == 1 else W))

        @pl.when(jnp.logical_not(top))
        def _():
            act(halo_copy(NE if d_lon == 1 else NW))

        @pl.when(jnp.logical_not(bottom))
        def _():
            act(halo_copy(SE if d_lon == 1 else SW))

    def start(copy):
        copy.start()

    @pl.when(last_lon)
    def _():
        halo_side(1, start)

    @pl.when(jnp.logical_not(first_lon))
    def _():
        halo_side(-1, start)

    @pl.when(jnp.logical_not(top))
    def _():
        halo_copy(N).start()

    @pl.when(jnp.logical_not(bottom))
    def _():
        halo_copy(S).start()

    def wanted(kind, to):
        low = q - to - 2 + 2 * n_lon
        return (low + ((kind - low) & (GROUP - 1))) & (n_lon - 1)

    def kind_of(place):
        return jnp.where(keeper, GROUP - 1 - place, place)

    def lowest(kind, g):
        return wanted(kind, g * GROUP + GROUP - 1) >> 2

    for copy in large:
        copy.wait()
    u_base = 0
    v_base = depth * rows
    edge_lat[0, pl.ds(0, depth), :] = tr[pl.ds(rows - 1, depth, stride=rows), :]
    edge_lat[0, pl.ds(depth, depth), :] = vel[pl.ds(v_base + rows - 1, depth, stride=rows), :]
    edge_lat[1, pl.ds(0, depth), :] = tr[pl.ds(0, depth, stride=rows), :]
    edge_lat[1, pl.ds(depth, depth), :] = vel[pl.ds(v_base, depth, stride=rows), :]

    def spread_copy(j):
        to = (t_relay, v_relay)[j]
        return remote(
            edge_lat.at[0, pl.ds(j * depth, depth)],
            slab.at[pl.ds(0, depth)],
            trac_send.at[j],
            trac_recv.at[4],
            {"lat": to},
        )

    def lat_copy(north):
        slot = 1 if north else 0
        return remote(
            edge_lat.at[0 if north else 1],
            halo_lat.at[slot],
            trac_send.at[0 if north else 2],
            trac_recv.at[slot],
            {"lat": lat_at(1 if north else -1)},
        )

    @pl.when(top)
    def _():
        spread_copy(0).start()
        spread_copy(1).start()

    @pl.when(jnp.logical_not(top))
    def _():
        lat_copy(True).start()

    @pl.when(jnp.logical_not(bottom))
    def _():
        lat_copy(False).start()

    half = lane8 >> 1

    def pack(l, carry):
        pt, pu = carry
        for g in range(2):
            item = l + depth * g
            here = half == jnp.full((8, cols), item, jnp.int32)
            at = pl.multiple_of(l * rows + 8 * g, 8)
            pt = jnp.where(here, pltpu.roll(tr[pl.ds(at, 8), :], 2 * item + 1, axis=1), pt)
            pu = jnp.where(here, pltpu.roll(vel[pl.ds(at, 8), :], 2 * item + 1, axis=1), pu)
        return pt, pu

    pt, pu = lax.fori_loop(
        0, depth, pack, (jnp.zeros((8, cols), jnp.float32), jnp.zeros((8, cols), jnp.float32)), unroll=4
    )
    edge_lon[pl.ds(0, 8), :] = pt
    edge_lon[pl.ds(8, 8), :] = pu

    def lon_copy(east):
        slot = 1 if east else 0
        return remote(
            edge_lon,
            halo_lon.at[slot],
            trac_send.at[3 if east else 4],
            trac_recv.at[2 + slot],
            {"lon": lon_at(1 if east else -1)},
        )

    def trac_wait(dst, sem):
        remote(dst, dst, trac_send.at[5], sem, {"lon": lon}).wait_recv()

    @pl.when(relay)
    def _():
        trac_wait(slab.at[pl.ds(0, depth)], trac_recv.at[4])
        hold_copy(depth).start()

    @pl.when(last_lon)
    def _():
        lon_copy(True).start()

    h_own = own[pl.ds(3 * rows, rows), :]

    def pivots(l, carry):
        c_up, p_up = carry
        wet_below = (jnp.full((rows, cols), (l + 1).astype(jnp.float32)) < h_own).astype(jnp.float32)
        c_down = vert[jnp.minimum(l, depth - 2)] * wet_below
        pivot = (1.0 + c_up + c_down) + c_up * p_up
        inv = 1.0 / pivot
        p_down = -c_down * inv
        at = pl.ds(pl.multiple_of(l * rows, rows), rows)
        cpl[at, :] = c_up
        rec[at, :] = inv
        prime[at, :] = p_down
        mix_rows[pl.ds(l, 1), :] = jnp.full((1, cols), horiz[l])
        return c_down, p_down

    zero = jnp.zeros((rows, cols), jnp.float32)
    lax.fori_loop(0, depth, pivots, (zero, zero), unroll=2)

    lane16 = lax.broadcasted_iota(jnp.int32, (rows, cols), 1)
    row16 = lax.broadcasted_iota(jnp.int32, (rows, cols), 0)
    last_col = lane16 == cols - 1
    first_col = lane16 == 0
    last_row = row16 == rows - 1
    first_row = row16 == 0
    h_e = jnp.where(last_col, 0.0, pltpu.roll(h_own, cols - 1, axis=1))
    h_n = jnp.where(last_row, 0.0, pltpu.roll(h_own, rows - 1, axis=0))

    def fluxes(l, carry):
        at = pl.ds(pl.multiple_of(l * rows, rows), rows)
        t = tr[at, :]
        u = vel[at, :]
        v = vel[pl.ds(pl.multiple_of(v_base + l * rows, rows), rows), :]
        m = horiz[l]
        level = jnp.full((rows, cols), l.astype(jnp.float32))
        wet = (level < h_own).astype(jnp.float32)
        wet_e = (level < h_e).astype(jnp.float32)
        wet_n = (level < h_n).astype(jnp.float32)
        t_e = pltpu.roll(t, cols - 1, axis=1)
        u_e = pltpu.roll(u, cols - 1, axis=1)
        f_e = wet * wet_e * (m * (t_e - t) - 0.25 * (u + u_e) * (t + t_e))
        f_w = pltpu.roll(f_e, 1, axis=1)
        t_n = pltpu.roll(t, rows - 1, axis=0)
        v_n = pltpu.roll(v, rows - 1, axis=0)
        f_n = wet * wet_n * (m * (t_n - t) - 0.25 * (v + v_n) * (t + t_n))
        f_s = pltpu.roll(f_n, 1, axis=0)
        step_ref[at, :] = wet * (t + ((f_e - f_w) + (f_n - f_s)))
        return carry

    lax.fori_loop(0, depth, fluxes, 0, unroll=4)

    @pl.when(jnp.logical_not(last_lon))
    def _():
        pl.semaphore_wait(hello.at[0], 3 + count(first_lon, 3))
        halo_side(1, start)
        lon_copy(True).start()

    @pl.when(first_lon)
    def _():
        halo_side(-1, start)

    lon_copy(False).start()

    def final_copy(e, size, dst, recv):
        return remote(
            pick.at[e, pl.ds(0, size)], dst, fin_send.at[e], recv, {"lat": n_lat - 1, "lon": group + e}
        )

    def forward_copy(out, slot, to, size):
        return remote(
            fwd_out.at[out, pl.ds(0, size)], fwd_in.at[slot, pl.ds(0, size)], fwd_send.at[out], fwd_recv.at[slot], {"lon": to}
        )

    def chain_copy(slot, size):
        return remote(
            fwd_in.at[slot, pl.ds(0, size)],
            fwd_in.at[slot - 1, pl.ds(0, size)],
            fwd_send.at[slot],
            fwd_recv.at[slot - 1],
            {"lon": lon + onward},
        )

    def chain_wait(slot, size):
        dst = fwd_in.at[slot, pl.ds(0, size)]
        remote(dst, dst, fwd_send.at[0], fwd_recv.at[slot], {"lon": partner(0)}).wait_recv()

    rise, fall = half_way + 1, half_way

    def serve(size, block, target):
        def send(e, carry):
            pick[e, pl.ds(0, size), :] = block(e)
            target(e)
            return carry

        lax.fori_loop(0, GROUP, send, 0)

    def to_top(e):
        @pl.when(e != me)
        def _():
            final_copy(e, block, fin.at[me], fin_recv.at[me]).start()

    def to_relayed(j):
        return lambda e: final_copy(e, depth, tfin.at[j, me], tfin_recv.at[j, me]).start()

    members = ((top, block, to_top), (is_t_relay, depth, to_relayed(0)), (is_v_relay, depth, to_relayed(1)))

    for role, size, target in members:

        @pl.when(role & keeper)
        def _(size=size, target=target):
            for g in range(n_group):
                dst = hold.at[g, pl.ds(0, size)]
                remote(dst, dst, hold_send.at[0], hold_recv.at[g], {"lon": partner(0)}).wait_recv()
            serve(size, lambda e: hold[wanted(GROUP - 1 - me, e) >> 2, pl.ds(0, size), :], target)

            first_up = lowest(GROUP - 1 - me, 1)
            first_down = lowest(GROUP - 1 - me, n_group - 1)

            def forward_up(j, carry):
                slot = (first_up + 1 - j + n_group) & (n_group - 1)
                fwd_out[j, pl.ds(0, size), :] = hold[slot, pl.ds(0, size), :]
                forward_copy(j, j, partner(1), size).start()
                return carry

            def forward_down(j, carry):
                slot = (first_down + j) & (n_group - 1)
                fwd_out[rise + j, pl.ds(0, size), :] = hold[slot, pl.ds(0, size), :]
                forward_copy(rise + j, j, partner(n_group - 1), size).start()
                return carry

            lax.fori_loop(0, rise, forward_up, 0)
            lax.fori_loop(0, fall, forward_down, 0)

    for side in (E, W):
        halo_wait(side)

    @pl.when(jnp.logical_not(top))
    def _():
        for side in (N, NE, NW):
            halo_wait(side)

    @pl.when(jnp.logical_not(bottom))
    def _():
        for side in (S, SE, SW):
            halo_wait(side)

    near = lane8 < cols // 2
    west_half, east_half = pl.ds(0, cols), pl.ds(cols, cols)

    low, high = SUB, SUB + rows

    def beside(east, west, base, first, last):
        for k in range(8):
            tile = jnp.where(
                near,
                pltpu.roll(side_in[east], (cols - 16 * k) % cols, axis=1),
                pltpu.roll(side_in[west], (cols - 16 - 16 * k) % cols, axis=1),
            )
            at = 8 * (k % 2)
            lo, hi = max(first, at), min(last, at + 8)
            ext[k // 2, pl.ds(base + lo - first, hi - lo), east_half] = tile[lo - at : hi - at]

    beside(SE, SW, 0, rows - SUB, rows)
    beside(E, W, low, 0, rows)
    for f in range(4):
        ext[f, pl.ds(0, SUB), west_half] = halo[1, pl.ds((f + 1) * rows - SUB, SUB), :]
        ext[f, pl.ds(low, rows), west_half] = own[pl.ds(f * rows, rows), :]
    fold_fix[...] = jnp.zeros((8, 2 * cols), jnp.float32)

    @pl.when(jnp.logical_not(top))
    def _():
        beside(NE, NW, high, 0, SUB)
        for f in range(4):
            ext[f, pl.ds(high, SUB), west_half] = halo[0, pl.ds(f * rows, SUB), :]

    trac_wait(halo_lon.at[0], trac_recv.at[2])
    trac_wait(halo_lon.at[1], trac_recv.at[3])

    @pl.when(jnp.logical_not(top))
    def _():
        trac_wait(halo_lat.at[0], trac_recv.at[0])

    @pl.when(jnp.logical_not(bottom))
    def _():
        trac_wait(halo_lat.at[1], trac_recv.at[1])

    even = (lane8 & 1) == 0
    h_beside = ext[3, pl.ds(low, rows), east_half]
    h_north_row = halo[0, pl.ds(3 * rows, 1), :]
    h_south_row = halo[1, pl.ds(4 * rows - 1, 1), :]

    def swap(from_east, from_west):
        return jnp.where(
            even, pltpu.roll(from_east, cols - 1, axis=1), pltpu.roll(from_west, 1, axis=1)
        )

    pt = edge_lon[pl.ds(0, 8), :]
    pu = edge_lon[pl.ds(8, 8), :]
    th = swap(halo_lon[0, pl.ds(0, 8), :], halo_lon[1, pl.ds(0, 8), :])
    uh = swap(halo_lon[0, pl.ds(8, 8), :], halo_lon[1, pl.ds(8, 8), :])

    def column(tile, at):
        lo = jnp.broadcast_to(tile[0:8, at : at + 1], (8, cols))
        hi = jnp.broadcast_to(tile[8:16, at : at + 1], (8, cols))
        return jnp.where(half < depth, lo, hi)

    level_of = (half & (depth - 1)).astype(jnp.float32)
    h_in = jnp.where(even, column(h_own, cols - 1), column(h_own, 0))
    h_out = jnp.where(even, column(h_beside, 0), column(h_beside, cols - 1))
    wet_pair = (level_of < h_in).astype(jnp.float32) * (level_of < h_out).astype(jnp.float32)

    def lane_mix(l, acc):
        return jnp.where((half & (depth - 1)) == jnp.full((8, cols), l, jnp.int32), horiz[l], acc)

    mix_lanes = lax.fori_loop(0, depth, lane_mix, jnp.zeros((8, cols), jnp.float32), unroll=4)
    sign = jnp.where(even, 1.0, -1.0)
    side_flux = wet_pair * (mix_lanes * (th - pt) - sign * (0.25 * (pu + uh) * (pt + th)))

    level_row = lax.broadcasted_iota(jnp.int32, (depth, cols), 0).astype(jnp.float32)

    def row_face(low_t, low_v, high_t, high_v, h_low, h_high):
        wet = (level_row < h_low).astype(jnp.float32) * (level_row < h_high).astype(jnp.float32)
        return wet * (mix_rows[...] * (high_t - low_t) - 0.25 * (low_v + high_v) * (low_t + high_t))

    first, second = pl.ds(0, depth), pl.ds(depth, depth)
    face_lat[0] = row_face(
        edge_lat[0, first, :], edge_lat[0, second, :], halo_lat[0, first, :], halo_lat[0, second, :],
        own[pl.ds(4 * rows - 1, 1), :], h_north_row,
    )
    face_lat[1] = row_face(
        halo_lat[1, first, :], halo_lat[1, second, :], edge_lat[1, first, :], edge_lat[1, second, :],
        h_south_row, own[pl.ds(3 * rows, 1), :],
    )

    rim_col = last_col | first_col

    def forward(l, sweep):
        at = pl.ds(pl.multiple_of(l * rows, rows), rows)
        rim = jnp.concatenate(
            [
                pltpu.roll(side_flux, cols - 1 - 2 * l, axis=1),
                pltpu.roll(side_flux, lax.rem(2 * cols - 1 - 2 * (l + depth), cols), axis=1),
            ],
            axis=0,
        )
        gain = jnp.where(rim_col, rim, 0.0) + (
            jnp.where(last_row, face_lat[0, pl.ds(l, 1), :], 0.0)
            - jnp.where(first_row, face_lat[1, pl.ds(l, 1), :], 0.0)
        )
        sweep = ((step_ref[at, :] + gain) + cpl[at, :] * sweep) * rec[at, :]
        step_ref[at, :] = sweep
        return sweep

    lax.fori_loop(0, depth, forward, zero, unroll=4)

    def backward(i, x):
        l = depth - 1 - i
        at = pl.ds(pl.multiple_of(l * rows, rows), rows)
        x = step_ref[at, :] - prime[at, :] * x
        tracer_out[at, :] = x
        return x

    lax.fori_loop(0, depth, backward, zero, unroll=4)

    for role, size, target in members:

        @pl.when(role & jnp.logical_not(keeper))
        def _(size=size, target=target):
            ring_hello()
            chain_wait(0, size)
            chain_wait(1, size)

            @pl.when(has_next)
            def _():
                chain_copy(1, size).start()

            first_slot = lowest(me, at_group)
            turned = jnp.where(rising, 1, 0)

            def either(e):
                which = ((wanted(me, group + e) >> 2) - first_slot + turned) & 1
                return jnp.where(
                    jnp.full((size, cols), which, jnp.int32) == 1,
                    fwd_in[1, pl.ds(0, size), :],
                    fwd_in[0, pl.ds(0, size), :],
                )

            serve(size, either, target)

            def hand_on(slot, carry):
                chain_wait(slot, size)
                chain_copy(slot, size).start()
                return carry

            lax.fori_loop(2, blocks, hand_on, 0)

    def source_of(shape, shift, isu):
        s = lax.broadcasted_iota(jnp.int32, shape, 1)
        l = (jnp.full(shape, r, jnp.int32) - isu - s) & (cols - 1)
        return s, l

    @pl.when(top)
    def _():
        shape = (block, cols)
        row = lax.broadcasted_iota(jnp.int32, shape, 0)
        isu = (((row >= 8) & (row < 16)) | ((row >= 24 + SUB) & (row < 16 + 2 * SUB))).astype(jnp.int32)
        s, l = source_of(shape, 0, isu)
        whole = n_lon * cols
        base = jnp.full(shape, pivot_col - lon * cols + 2 * whole, jnp.int32) - isu
        dev_main = ((base - l) & (whole - 1)) >> 7
        off = jnp.where(l < cols // 2, cols, -cols)
        dev_side = ((base - l - off) & (whole - 1)) >> 7
        main = jnp.zeros(shape, jnp.float32)
        side = main
        for e in range(GROUP):
            @pl.when(e != me)
            def _():
                trac_wait(fin.at[e], fin_recv.at[e])

            @pl.when(e == me)
            def _():
                fin[e] = pick[e]

        for e in range(GROUP):
            got = fin[e]
            src = jnp.full(shape, wanted(kind_of(e), lon), jnp.int32)
            main = jnp.where(dev_main == src, got, main)
            side = jnp.where(dev_side == src, got, side)
        main = jnp.take_along_axis(main, l, axis=1)
        side = jnp.take_along_axis(side, l, axis=1)
        for f in range(4):
            ff = (0, 1, 3, 2)[f]
            rest = 32 + (SUB - 8) * f
            for half_of, part in ((west_half, main), (east_half, side)):
                ext[ff, pl.ds(high, 8), half_of] = part[8 * f : 8 * f + 8]
                ext[ff, pl.ds(high + 8, SUB - 8), half_of] = part[rest : rest + SUB - 8]
        for half_of, part in ((west_half, main), (east_half, side)):
            fold_fix[pl.ds(high - 24, 1), half_of] = part[block - 8 : block - 7] - ext[2, pl.ds(high - 1, 1), half_of]

    wide = 2 * cols
    tall = rows + 2 * SUB
    h = ext[3]
    sea = (h > 0.0).astype(jnp.float32)

    def east(x):
        return pltpu.roll(x, wide - 1, axis=1)

    def north(x):
        return pltpu.roll(x, tall - 1, axis=0)

    zonal_mask = sea * east(sea)
    merid_mask = sea * north(sea)
    coef[0] = fb_step * ((h + east(h)) / (2.0 * depth)) * zonal_mask
    coef[1] = (1.0 - drag_rate) * zonal_mask
    coef[2] = fb_step * ((h + north(h)) / (2.0 * depth)) * merid_mask
    coef[3] = (1.0 - drag_rate) * merid_mask
    coef[4] = fb_step * sea
    coef[5] = pltpu.roll(coef[0], 1, axis=1)
    coef[6] = pltpu.roll(coef[1], 1, axis=1)
    coef[7] = pltpu.roll(coef[2], 1, axis=0)
    coef[8] = pltpu.roll(coef[3], 1, axis=0)

    def west(x):
        return pltpu.roll(x, 1, axis=1)

    def south(x):
        return pltpu.roll(x, 1, axis=0)

    def cycle(i, state):
        eta, u, u_west, v, v_south = state
        eta = eta - coef[4] * ((u - u_west) + (v - v_south))
        u = u * coef[1] - coef[0] * (east(eta) - eta)
        v = v * coef[3] - coef[2] * (north(eta) - eta)
        u_west = u_west * coef[6] - coef[5] * (eta - west(eta))
        v_south = v_south * coef[8] - coef[7] * (eta - south(eta))
        return eta, u, u_west, v, v_south

    v_south = south(ext[2])
    v_south = jnp.concatenate([v_south[:24], v_south[24:32] + fold_fix[...], v_south[32:]], axis=0)
    eta, u, _, v, _ = lax.fori_loop(0, SUB, cycle, (ext[0] * sea, ext[1], west(ext[1]), ext[2], v_south))
    surface_out[...] = eta[low:high, :cols]
    transport_out[pl.ds(0, rows), :] = u[low:high, :cols]
    transport_out[pl.ds(rows, rows), :] = v[low:high, :cols]

    @pl.when(top)
    def _():
        got = []
        for j in range(2):
            shape = (depth, cols)
            s, l = source_of(shape, 0, 0)
            whole = n_lon * cols
            dev = ((jnp.full(shape, pivot_col - lon * cols + 2 * whole, jnp.int32) - l) & (whole - 1)) >> 7
            acc = jnp.zeros(shape, jnp.float32)
            for e in range(GROUP):
                trac_wait(tfin.at[j, e], tfin_recv.at[j, e])
                acc = jnp.where(dev == jnp.full(shape, wanted(kind_of(e), lon), jnp.int32), tfin[j, e], acc)
            got.append(jnp.take_along_axis(acc, l, axis=1))
        h_last = own[pl.ds(4 * rows - 1, 1), :]
        flux = row_face(
            edge_lat[0, first, :], edge_lat[0, second, :], got[0], got[1], h_last, ext[3, pl.ds(high, 1), west_half]
        )
        face_lat[0] = (level_row < h_last).astype(jnp.float32) * flux
        c_last = cpl[pl.ds(rows - 1, depth, stride=rows), :]
        r_last = rec[pl.ds(rows - 1, depth, stride=rows), :]
        p_last = prime[pl.ds(rows - 1, depth, stride=rows), :]
        out_last = tracer_out[pl.ds(rows - 1, depth, stride=rows), :]
        delta = face_lat[0]
        sweeps = []
        x = jnp.zeros((1, cols), jnp.float32)
        for k in range(depth):
            x = (delta[k : k + 1] + c_last[k : k + 1] * x) * r_last[k : k + 1]
            sweeps.append(x)
        x = jnp.zeros((1, cols), jnp.float32)
        for k in range(depth - 1, -1, -1):
            x = sweeps[k] - p_last[k : k + 1] * x
            tracer_out[pl.ds(k * rows + rows - 1, 1), :] = out_last[k : k + 1] + x

    for side in (E, W):
        halo_copy(side).wait_send()
    lon_copy(True).wait_send()
    lon_copy(False).wait_send()

    @pl.when(jnp.logical_not(top))
    def _():
        for side in (N, NE, NW):
            halo_copy(side).wait_send()
        lat_copy(True).wait_send()

    @pl.when(jnp.logical_not(bottom))
    def _():
        for side in (S, SE, SW):
            halo_copy(side).wait_send()
        lat_copy(False).wait_send()

    @pl.when(top)
    def _():
        spread_copy(0).wait_send()
        spread_copy(1).wait_send()

        hold_copy(block).wait_send()

        @pl.when(keeper)
        def _():
            for j in range(rise):
                forward_copy(j, j, partner(1), block).wait_send()
            for j in range(fall):
                forward_copy(rise + j, j, partner(n_group - 1), block).wait_send()

        @pl.when(has_next)
        def _():
            def gone(slot, carry):
                chain_copy(slot, block).wait_send()
                return carry

            lax.fori_loop(1, blocks, gone, 0)

        for e in range(GROUP):

            @pl.when(e != me)
            def _(e=e):
                final_copy(e, block, fin.at[me], fin_recv.at[me]).wait_send()

    @pl.when(relay)
    def _():
        hold_copy(depth).wait_send()

        @pl.when(keeper)
        def _():
            for j in range(rise):
                forward_copy(j, j, partner(1), depth).wait_send()
            for j in range(fall):
                forward_copy(rise + j, j, partner(n_group - 1), depth).wait_send()

        @pl.when(has_next)
        def _():
            def gone(slot, carry):
                chain_copy(slot, depth).wait_send()
                return carry

            lax.fori_loop(1, blocks, gone, 0)

        for e in range(GROUP):
            final_copy(e, depth, tfin.at[0, me], tfin_recv.at[0, me]).wait_send()


def write_out(a, b, c, a_hbm, b_hbm, c_hbm, sem):
    copies = [
        pltpu.make_async_copy(src, dst, sem.at[i])
        for i, (src, dst) in enumerate(((a, a_hbm), (b, b_hbm), (c, c_hbm)))
    ]
    for copy in copies:
        copy.start()
    for copy in copies:
        copy.wait()


def solution(mesh):
    n_lon, n_lat = mesh.shape["lon"], mesh.shape["lat"]

    def shards(tracer, velocity, surface, transport, horiz_mixing, vert_mixing, levels, land_tiles, fold_pair):
        depth, rows, cols = tracer.shape
        f32 = jnp.float32
        hbm = pl.BlockSpec(memory_space=pl.ANY)
        vmem = pl.BlockSpec(memory_space=pltpu.VMEM)
        dma = pltpu.SemaphoreType.DMA
        field = pltpu.VMEM((depth * rows, cols), f32)
        results = pl.pallas_call(
            functools.partial(ocean_kernel, n_lon, n_lat, depth, rows, cols),
            name="ocean",
            out_shape=(
                pltpu.VMEM((depth * rows, cols), f32),
                pltpu.VMEM((rows, cols), f32),
                pltpu.VMEM((2 * rows, cols), f32),
            ),
            in_specs=[hbm] * 9,
            out_specs=(vmem, vmem, vmem),
            scratch_shapes=[
                pltpu.SMEM((depth,), f32),
                pltpu.SMEM((depth - 1,), f32),
                pltpu.SMEM((1, 1), jnp.int32),
                pltpu.SMEM((cols,), jnp.int32),
                field,
                pltpu.VMEM((2 * depth * rows, cols), f32),
                pltpu.VMEM((rows, cols), jnp.int32),
                pltpu.VMEM((4 * rows, cols), f32),
                pltpu.VMEM((2, 4 * rows, cols), f32),
                pltpu.VMEM((2, 8, cols), f32),
                pltpu.VMEM((8, 8, cols), f32),
                pltpu.VMEM((16, cols), f32),
                pltpu.VMEM((2, 16, cols), f32),
                pltpu.VMEM((2, 2 * depth, cols), f32),
                pltpu.VMEM((2, 2 * depth, cols), f32),
                pltpu.VMEM((4 * SUB + 8, cols), f32),
                pltpu.VMEM((n_lon // GROUP, 4 * SUB + 8, cols), f32),
                pltpu.VMEM((n_lon // GROUP + 1, 4 * SUB + 8, cols), f32),
                pltpu.VMEM((n_lon // GROUP // 2 + 1, 4 * SUB + 8, cols), f32),
                pltpu.VMEM((GROUP, 4 * SUB + 8, cols), f32),
                pltpu.VMEM((GROUP, 4 * SUB + 8, cols), f32),
                pltpu.VMEM((2, GROUP, depth, cols), f32),
                field,
                field,
                field,
                field,
                pltpu.VMEM((2, depth, cols), f32),
                pltpu.VMEM((depth, cols), f32),
                pltpu.VMEM((4, rows + 2 * SUB, 2 * cols), f32),
                pltpu.VMEM((9, rows + 2 * SUB, 2 * cols), f32),
                pltpu.VMEM((8, 2 * cols), f32),
                dma((9,)),
                pltpu.SemaphoreType.REGULAR((2,)),
                dma((8,)),
                dma((8,)),
                dma((6,)),
                dma((5,)),
                dma((1,)),
                dma((n_lon // GROUP,)),
                dma((n_lon // GROUP + 1,)),
                dma((n_lon // GROUP // 2 + 1,)),
                dma((GROUP,)),
                dma((GROUP,)),
                dma((2, GROUP)),
            ],
            compiler_params=pltpu.CompilerParams(collective_id=1, has_side_effects=True),
        )(
            tracer.reshape(depth * rows, cols),
            velocity.reshape(2 * depth * rows, cols),
            surface,
            transport.reshape(2 * rows, cols),
            levels,
            horiz_mixing,
            vert_mixing,
            land_tiles,
            fold_pair,
        )
        results = [pltpu.with_memory_space_constraint(result, pltpu.VMEM) for result in results]
        tracer_new, surface_new, transport_new = pl.pallas_call(
            write_out,
            name="write_out",
            out_shape=tuple(jax.ShapeDtypeStruct(result.shape, f32) for result in results),
            in_specs=[vmem] * 3,
            out_specs=(hbm,) * 3,
            scratch_shapes=[dma((3,))],
        )(*results)
        return (
            tracer_new.reshape(depth, rows, cols),
            surface_new,
            transport_new.reshape(2, rows, cols),
        )

    return jax.shard_map(
        shards,
        mesh=mesh,
        in_specs=(
            P("member", "lat", "lon"),
            P(None, "member", "lat", "lon"),
            P(("member", "lat"), "lon"),
            P("member", "lat", "lon"),
            P("member"),
            P("member"),
            P("lat", "lon"),
            P("lat", "lon"),
            P("lon"),
        ),
        out_specs=(
            P("member", "lat", "lon"),
            P(("member", "lat"), "lon"),
            P("member", "lat", "lon"),
        ),
        check_vma=False,
    )
```

```python
import functools

import jax
import jax.numpy as jnp
from jax import lax
from jax.experimental import pallas as pl
from jax.experimental.pallas import tpu as pltpu
from jax.sharding import PartitionSpec as P

SUB = 12
fb_step = 0.6
drag_rate = 0.02
MESH = pl.DeviceIdType.MESH

E, W, N, S, NE, NW, SE, SW = range(8)
OPPOSITE = {E: W, W: E, N: S, S: N, NE: SW, SW: NE, NW: SE, SE: NW}
STEP = {E: (0, 1), W: (0, -1), N: (1, 0), S: (-1, 0), NE: (1, 1), NW: (1, -1), SE: (-1, 1), SW: (-1, -1)}
GROUP = 4


def ocean_kernel(
    n_lon,
    n_lat,
    depth,
    rows,
    cols,
    tracer_hbm,
    velocity_hbm,
    surface_hbm,
    transport_hbm,
    levels_hbm,
    horiz_hbm,
    vert_hbm,
    land_hbm,
    fold_hbm,
    tracer_out,
    surface_out,
    transport_out,
    horiz,
    vert,
    land,
    fold,
    tr,
    vel,
    lev,
    own,
    halo,
    side_out,
    side_in,
    edge_lon,
    halo_lon,
    edge_lat,
    halo_lat,
    slab,
    hold,
    fwd_out,
    fwd_in,
    pick,
    fin,
    tfin,
    step_ref,
    cpl,
    rec,
    prime,
    face_lat,
    mix_rows,
    ext,
    coef,
    fold_fix,
    load_sem,
    hello,
    halo_send,
    halo_recv,
    trac_send,
    trac_recv,
    hold_send,
    hold_recv,
    fwd_send,
    fwd_recv,
    fin_send,
    fin_recv,
    tfin_recv,
):
    lat = lax.axis_index("lat")
    lon = lax.axis_index("lon")
    top = lat == n_lat - 1
    bottom = lat == 0
    t_relay = n_lat - 3
    v_relay = 1
    is_t_relay = lat == t_relay
    is_v_relay = lat == v_relay
    relay = is_t_relay | is_v_relay
    ring = top | relay
    n_group = n_lon // GROUP
    me = lon & (GROUP - 1)
    group = lon - me
    keeper = lon < GROUP
    block = 4 * SUB + 8
    half_way = n_group // 2
    at_group = lon >> 2
    rising = at_group <= half_way
    blocks = jnp.where(rising, half_way + 2 - at_group, half_way + 1 - n_group + at_group)
    onward = jnp.where(rising, GROUP, -GROUP)
    has_next = jnp.logical_not(keeper) & (blocks > 2)
    has_previous = (at_group > 1) & (at_group < n_group - 1)

    def partner(g):
        return g * GROUP + (GROUP - 1 - me)

    def lon_at(step):
        return lax.rem(lon + step + n_lon, n_lon)

    def lat_at(step):
        return lax.rem(lat + step + n_lat, n_lat)

    def remote(src, dst, send, recv, to):
        return pltpu.make_async_remote_copy(
            src_ref=src, dst_ref=dst, send_sem=send, recv_sem=recv, device_id=to, device_id_type=MESH
        )

    small = [
        pltpu.make_async_copy(surface_hbm, own.at[pl.ds(0, rows)], load_sem.at[0]),
        pltpu.make_async_copy(transport_hbm, own.at[pl.ds(rows, 2 * rows)], load_sem.at[1]),
        pltpu.make_async_copy(levels_hbm, lev, load_sem.at[2]),
        pltpu.make_async_copy(land_hbm, land, load_sem.at[5]),
        pltpu.make_async_copy(fold_hbm, fold, load_sem.at[6]),
        pltpu.make_async_copy(horiz_hbm, horiz, load_sem.at[7]),
        pltpu.make_async_copy(vert_hbm, vert, load_sem.at[8]),
    ]
    large = [
        pltpu.make_async_copy(tracer_hbm, tr, load_sem.at[3]),
        pltpu.make_async_copy(velocity_hbm, vel, load_sem.at[4]),
    ]
    for copy in small:
        copy.start()
    barrier = pltpu.get_barrier_semaphore()

    def signal(sem, d_lat, to):
        pl.semaphore_signal(
            sem, inc=1, device_id={"lat": lat_at(d_lat), "lon": to}, device_id_type=MESH
        )

    first_lon, last_lon = lon == 0, lon == n_lon - 1

    def signal_side(sem, d_lon):
        for d_lat in (-1, 0, 1):
            signal(sem, d_lat, lon_at(d_lon))

    for d_lat in (-2, -1, 1, 2):
        signal(barrier, d_lat, lon)

    @pl.when(jnp.logical_not(last_lon))
    def _():
        signal_side(barrier, 1)

    @pl.when(first_lon)
    def _():
        signal_side(barrier, -1)

    @pl.when(ring)
    def _():
        @pl.when(keeper)
        def _():
            for g in range(1, n_group):
                signal(barrier, 0, partner(g))

        @pl.when(has_previous & jnp.logical_not(rising))
        def _():
            signal(barrier, 0, lon - onward)

        @pl.when(has_next & rising)
        def _():
            signal(barrier, 0, lon + onward)

        for place in range(1, GROUP):

            @pl.when(place > me)
            def _(place=place):
                signal(barrier, 0, group + place)

    for copy in large:
        copy.start()

    zeros_tile = jnp.zeros((4 * rows, cols), jnp.float32)

    @pl.when(bottom)
    def _():
        halo[1] = zeros_tile
        for side in (SE, SW):
            side_in[side] = jnp.zeros((8, cols), jnp.float32)
        halo_lat[1] = jnp.zeros((2 * depth, cols), jnp.float32)

    @pl.when(top)
    def _():
        halo[0] = zeros_tile
        for side in (NE, NW):
            side_in[side] = jnp.zeros((8, cols), jnp.float32)
        halo_lat[0] = jnp.zeros((2 * depth, cols), jnp.float32)

    for copy in small[:4]:
        copy.wait()
    dry = 1 - land[0, 0]
    own[pl.ds(3 * rows, rows), :] = (lev[...] * dry).astype(jnp.float32)

    lane8 = lax.broadcasted_iota(jnp.int32, (8, cols), 1)
    to_east, to_west = jnp.zeros((8, cols), jnp.float32), jnp.zeros((8, cols), jnp.float32)
    for k in range(8):
        here = (lane8 >> 4) == k
        part = own[pl.ds(8 * k, 8), :]
        to_east = jnp.where(here, pltpu.roll(part, (16 * k + 16) % cols, axis=1), to_east)
        to_west = jnp.where(here, pltpu.roll(part, 16 * k, axis=1) if k else part, to_west)
    side_out[0] = to_east
    side_out[1] = to_west

    @pl.when(top)
    def _():
        slab[pl.ds(block - 8, 8), :] = jnp.zeros((8, cols), jnp.float32)
        for f, (start, back, sign) in enumerate(((0, 0, 1), (rows, 0, -1), (3 * rows, 0, 1), (2 * rows, 1, -1))):
            for i in range(SUB):
                row = own[pl.ds(start + rows - 1 - i - back, 1), :]
                at = 8 * f + i if i < 8 else 32 + (SUB - 8) * f + i - 8
                slab[pl.ds(at, 1), :] = row if sign == 1 else -row
        slab[pl.ds(block - 8, 1), :] = -own[pl.ds(3 * rows - 1, 1), :]

    def count(flag, n=1):
        return jnp.where(flag, n, 0)

    chained = (rising & has_previous) | (jnp.logical_not(rising) & has_next)
    lower_ring = me + count(jnp.logical_not(keeper)) + count(chained)
    pl.semaphore_wait(barrier, 4 + count(jnp.logical_not(first_lon), 3) + count(last_lon, 3) + count(ring, lower_ring))

    @pl.when(jnp.logical_not(first_lon))
    def _():
        signal_side(hello.at[0], -1)

    @pl.when(last_lon)
    def _():
        signal_side(hello.at[0], 1)

    @pl.when(ring)
    def _():
        for place in range(GROUP - 1):

            @pl.when(place < me)
            def _(place=place):
                signal(hello.at[1], 0, group + place)

        @pl.when(has_previous & rising)
        def _():
            signal(hello.at[1], 0, lon - onward)

    def ring_hello():
        later = GROUP - 1 - me + count(has_next & rising)

        @pl.when(later > 0)
        def _():
            pl.semaphore_wait(hello.at[1], later)

    @pl.when(ring & keeper)
    def _():
        ring_hello()

    def hold_copy(size):
        slot = lon >> 2
        return remote(
            slab.at[pl.ds(0, size)],
            hold.at[slot, pl.ds(0, size)],
            hold_send.at[0],
            hold_recv.at[slot],
            {"lon": partner(0)},
        )

    @pl.when(top)
    def _():
        hold_copy(block).start()

    for copy in small[4:]:
        copy.wait()
    pivot_col = lax.rem(fold[0] + lon * cols, n_lon * cols)
    q = lax.div(pivot_col, cols)
    r = lax.rem(pivot_col, cols)

    def halo_copy(side):
        d_lat, d_lon = STEP[side]
        slot = OPPOSITE[side]
        if d_lon == 0:
            src, dst = own, halo.at[0 if slot == N else 1]
        else:
            src, dst = side_out.at[0 if d_lon == 1 else 1], side_in.at[slot]
        return remote(
            src,
            dst,
            halo_send.at[side],
            halo_recv.at[slot],
            {"lat": lat_at(d_lat), "lon": lon_at(d_lon)},
        )

    def halo_wait(side):
        dst = halo.at[0 if side == N else 1] if side in (N, S) else side_in.at[side]
        remote(dst, dst, halo_send.at[side], halo_recv.at[side], {"lon": lon}).wait_recv()

    def halo_side(d_lon, act):
        act(halo_copy(E if d_lon == 1 else W))

        @pl.when(jnp.logical_not(top))
        def _():
            act(halo_copy(NE if d_lon == 1 else NW))

        @pl.when(jnp.logical_not(bottom))
        def _():
            act(halo_copy(SE if d_lon == 1 else SW))

    def start(copy):
        copy.start()

    @pl.when(last_lon)
    def _():
        halo_side(1, start)

    @pl.when(jnp.logical_not(first_lon))
    def _():
        halo_side(-1, start)

    @pl.when(jnp.logical_not(top))
    def _():
        halo_copy(N).start()

    @pl.when(jnp.logical_not(bottom))
    def _():
        halo_copy(S).start()

    def wanted(kind, to):
        low = q - to - 2 + 2 * n_lon
        return (low + ((kind - low) & (GROUP - 1))) & (n_lon - 1)

    def kind_of(place):
        return jnp.where(keeper, GROUP - 1 - place, place)

    def lowest(kind, g):
        return wanted(kind, g * GROUP + GROUP - 1) >> 2

    for copy in large:
        copy.wait()
    u_base = 0
    v_base = depth * rows
    edge_lat[0, pl.ds(0, depth), :] = tr[pl.ds(rows - 1, depth, stride=rows), :]
    edge_lat[0, pl.ds(depth, depth), :] = vel[pl.ds(v_base + rows - 1, depth, stride=rows), :]
    edge_lat[1, pl.ds(0, depth), :] = tr[pl.ds(0, depth, stride=rows), :]
    edge_lat[1, pl.ds(depth, depth), :] = vel[pl.ds(v_base, depth, stride=rows), :]

    def spread_copy(j):
        to = (t_relay, v_relay)[j]
        return remote(
            edge_lat.at[0, pl.ds(j * depth, depth)],
            slab.at[pl.ds(0, depth)],
            trac_send.at[j],
            trac_recv.at[4],
            {"lat": to},
        )

    def lat_copy(north):
        slot = 1 if north else 0
        return remote(
            edge_lat.at[0 if north else 1],
            halo_lat.at[slot],
            trac_send.at[0 if north else 2],
            trac_recv.at[slot],
            {"lat": lat_at(1 if north else -1)},
        )

    @pl.when(top)
    def _():
        spread_copy(0).start()
        spread_copy(1).start()

    @pl.when(jnp.logical_not(top))
    def _():
        lat_copy(True).start()

    @pl.when(jnp.logical_not(bottom))
    def _():
        lat_copy(False).start()

    half = lane8 >> 1

    def pack(l, carry):
        pt, pu = carry
        for g in range(2):
            item = l + depth * g
            here = half == jnp.full((8, cols), item, jnp.int32)
            at = pl.multiple_of(l * rows + 8 * g, 8)
            pt = jnp.where(here, pltpu.roll(tr[pl.ds(at, 8), :], 2 * item + 1, axis=1), pt)
            pu = jnp.where(here, pltpu.roll(vel[pl.ds(at, 8), :], 2 * item + 1, axis=1), pu)
        return pt, pu

    pt, pu = lax.fori_loop(
        0, depth, pack, (jnp.zeros((8, cols), jnp.float32), jnp.zeros((8, cols), jnp.float32)), unroll=4
    )
    edge_lon[pl.ds(0, 8), :] = pt
    edge_lon[pl.ds(8, 8), :] = pu

    def lon_copy(east):
        slot = 1 if east else 0
        return remote(
            edge_lon,
            halo_lon.at[slot],
            trac_send.at[3 if east else 4],
            trac_recv.at[2 + slot],
            {"lon": lon_at(1 if east else -1)},
        )

    def trac_wait(dst, sem):
        remote(dst, dst, trac_send.at[5], sem, {"lon": lon}).wait_recv()

    @pl.when(relay)
    def _():
        trac_wait(slab.at[pl.ds(0, depth)], trac_recv.at[4])
        hold_copy(depth).start()

    @pl.when(last_lon)
    def _():
        lon_copy(True).start()

    h_own = own[pl.ds(3 * rows, rows), :]

    def pivots(l, carry):
        c_up, p_up = carry
        wet_below = (jnp.full((rows, cols), (l + 1).astype(jnp.float32)) < h_own).astype(jnp.float32)
        c_down = vert[jnp.minimum(l, depth - 2)] * wet_below
        pivot = (1.0 + c_up + c_down) + c_up * p_up
        inv = 1.0 / pivot
        p_down = -c_down * inv
        at = pl.ds(pl.multiple_of(l * rows, rows), rows)
        cpl[at, :] = c_up
        rec[at, :] = inv
        prime[at, :] = p_down
        mix_rows[pl.ds(l, 1), :] = jnp.full((1, cols), horiz[l])
        return c_down, p_down

    zero = jnp.zeros((rows, cols), jnp.float32)
    lax.fori_loop(0, depth, pivots, (zero, zero), unroll=2)

    lane16 = lax.broadcasted_iota(jnp.int32, (rows, cols), 1)
    row16 = lax.broadcasted_iota(jnp.int32, (rows, cols), 0)
    last_col = lane16 == cols - 1
    first_col = lane16 == 0
    last_row = row16 == rows - 1
    first_row = row16 == 0
    h_e = jnp.where(last_col, 0.0, pltpu.roll(h_own, cols - 1, axis=1))
    h_n = jnp.where(last_row, 0.0, pltpu.roll(h_own, rows - 1, axis=0))

    def fluxes(l, carry):
        at = pl.ds(pl.multiple_of(l * rows, rows), rows)
        t = tr[at, :]
        u = vel[at, :]
        v = vel[pl.ds(pl.multiple_of(v_base + l * rows, rows), rows), :]
        m = horiz[l]
        level = jnp.full((rows, cols), l.astype(jnp.float32))
        wet = (level < h_own).astype(jnp.float32)
        wet_e = (level < h_e).astype(jnp.float32)
        wet_n = (level < h_n).astype(jnp.float32)
        t_e = pltpu.roll(t, cols - 1, axis=1)
        u_e = pltpu.roll(u, cols - 1, axis=1)
        f_e = wet * wet_e * (m * (t_e - t) - 0.25 * (u + u_e) * (t + t_e))
        f_w = pltpu.roll(f_e, 1, axis=1)
        t_n = pltpu.roll(t, rows - 1, axis=0)
        v_n = pltpu.roll(v, rows - 1, axis=0)
        f_n = wet * wet_n * (m * (t_n - t) - 0.25 * (v + v_n) * (t + t_n))
        f_s = pltpu.roll(f_n, 1, axis=0)
        step_ref[at, :] = wet * (t + ((f_e - f_w) + (f_n - f_s)))
        return carry

    lax.fori_loop(0, depth, fluxes, 0, unroll=4)

    @pl.when(jnp.logical_not(last_lon))
    def _():
        pl.semaphore_wait(hello.at[0], 3 + count(first_lon, 3))
        halo_side(1, start)
        lon_copy(True).start()

    @pl.when(first_lon)
    def _():
        halo_side(-1, start)

    lon_copy(False).start()

    def final_copy(e, size, dst, recv):
        return remote(
            pick.at[e, pl.ds(0, size)], dst, fin_send.at[e], recv, {"lat": n_lat - 1, "lon": group + e}
        )

    def forward_copy(out, slot, to, size):
        return remote(
            fwd_out.at[out, pl.ds(0, size)], fwd_in.at[slot, pl.ds(0, size)], fwd_send.at[out], fwd_recv.at[slot], {"lon": to}
        )

    def chain_copy(slot, size):
        return remote(
            fwd_in.at[slot, pl.ds(0, size)],
            fwd_in.at[slot - 1, pl.ds(0, size)],
            fwd_send.at[slot],
            fwd_recv.at[slot - 1],
            {"lon": lon + onward},
        )

    def chain_wait(slot, size):
        dst = fwd_in.at[slot, pl.ds(0, size)]
        remote(dst, dst, fwd_send.at[0], fwd_recv.at[slot], {"lon": partner(0)}).wait_recv()

    rise, fall = half_way + 1, half_way

    def serve(size, block, target):
        def send(e, carry):
            pick[e, pl.ds(0, size), :] = block(e)
            target(e)
            return carry

        lax.fori_loop(0, GROUP, send, 0)

    def to_top(e):
        @pl.when(e != me)
        def _():
            final_copy(e, block, fin.at[me], fin_recv.at[me]).start()

    def to_relayed(j):
        return lambda e: final_copy(e, depth, tfin.at[j, me], tfin_recv.at[j, me]).start()

    members = ((top, block, to_top), (is_t_relay, depth, to_relayed(0)), (is_v_relay, depth, to_relayed(1)))

    for role, size, target in members:

        @pl.when(role & keeper)
        def _(size=size, target=target):
            for g in range(n_group):
                dst = hold.at[g, pl.ds(0, size)]
                remote(dst, dst, hold_send.at[0], hold_recv.at[g], {"lon": partner(0)}).wait_recv()
            serve(size, lambda e: hold[wanted(GROUP - 1 - me, e) >> 2, pl.ds(0, size), :], target)

            first_up = lowest(GROUP - 1 - me, 1)
            first_down = lowest(GROUP - 1 - me, n_group - 1)

            def forward_up(j, carry):
                slot = (first_up + 1 - j + n_group) & (n_group - 1)
                fwd_out[j, pl.ds(0, size), :] = hold[slot, pl.ds(0, size), :]
                forward_copy(j, j, partner(1), size).start()
                return carry

            def forward_down(j, carry):
                slot = (first_down + j) & (n_group - 1)
                fwd_out[rise + j, pl.ds(0, size), :] = hold[slot, pl.ds(0, size), :]
                forward_copy(rise + j, j, partner(n_group - 1), size).start()
                return carry

            lax.fori_loop(0, rise, forward_up, 0)
            lax.fori_loop(0, fall, forward_down, 0)

    for side in (E, W):
        halo_wait(side)

    @pl.when(jnp.logical_not(top))
    def _():
        for side in (N, NE, NW):
            halo_wait(side)

    @pl.when(jnp.logical_not(bottom))
    def _():
        for side in (S, SE, SW):
            halo_wait(side)

    near = lane8 < cols // 2
    west_half, east_half = pl.ds(0, cols), pl.ds(cols, cols)

    low, high = SUB, SUB + rows

    def beside(east, west, base, first, last):
        for k in range(8):
            tile = jnp.where(
                near,
                pltpu.roll(side_in[east], (cols - 16 * k) % cols, axis=1),
                pltpu.roll(side_in[west], (cols - 16 - 16 * k) % cols, axis=1),
            )
            at = 8 * (k % 2)
            lo, hi = max(first, at), min(last, at + 8)
            ext[k // 2, pl.ds(base + lo - first, hi - lo), east_half] = tile[lo - at : hi - at]

    beside(SE, SW, 0, rows - SUB, rows)
    beside(E, W, low, 0, rows)
    for f in range(4):
        ext[f, pl.ds(0, SUB), west_half] = halo[1, pl.ds((f + 1) * rows - SUB, SUB), :]
        ext[f, pl.ds(low, rows), west_half] = own[pl.ds(f * rows, rows), :]
    fold_fix[...] = jnp.zeros((8, 2 * cols), jnp.float32)

    @pl.when(jnp.logical_not(top))
    def _():
        beside(NE, NW, high, 0, SUB)
        for f in range(4):
            ext[f, pl.ds(high, SUB), west_half] = halo[0, pl.ds(f * rows, SUB), :]

    trac_wait(halo_lon.at[0], trac_recv.at[2])
    trac_wait(halo_lon.at[1], trac_recv.at[3])

    @pl.when(jnp.logical_not(top))
    def _():
        trac_wait(halo_lat.at[0], trac_recv.at[0])

    @pl.when(jnp.logical_not(bottom))
    def _():
        trac_wait(halo_lat.at[1], trac_recv.at[1])

    even = (lane8 & 1) == 0
    h_beside = ext[3, pl.ds(low, rows), east_half]
    h_north_row = halo[0, pl.ds(3 * rows, 1), :]
    h_south_row = halo[1, pl.ds(4 * rows - 1, 1), :]

    def swap(from_east, from_west):
        return jnp.where(
            even, pltpu.roll(from_east, cols - 1, axis=1), pltpu.roll(from_west, 1, axis=1)
        )

    pt = edge_lon[pl.ds(0, 8), :]
    pu = edge_lon[pl.ds(8, 8), :]
    th = swap(halo_lon[0, pl.ds(0, 8), :], halo_lon[1, pl.ds(0, 8), :])
    uh = swap(halo_lon[0, pl.ds(8, 8), :], halo_lon[1, pl.ds(8, 8), :])

    def column(tile, at):
        lo = jnp.broadcast_to(tile[0:8, at : at + 1], (8, cols))
        hi = jnp.broadcast_to(tile[8:16, at : at + 1], (8, cols))
        return jnp.where(half < depth, lo, hi)

    level_of = (half & (depth - 1)).astype(jnp.float32)
    h_in = jnp.where(even, column(h_own, cols - 1), column(h_own, 0))
    h_out = jnp.where(even, column(h_beside, 0), column(h_beside, cols - 1))
    wet_pair = (level_of < h_in).astype(jnp.float32) * (level_of < h_out).astype(jnp.float32)

    def lane_mix(l, acc):
        return jnp.where((half & (depth - 1)) == jnp.full((8, cols), l, jnp.int32), horiz[l], acc)

    mix_lanes = lax.fori_loop(0, depth, lane_mix, jnp.zeros((8, cols), jnp.float32), unroll=4)
    sign = jnp.where(even, 1.0, -1.0)
    side_flux = wet_pair * (mix_lanes * (th - pt) - sign * (0.25 * (pu + uh) * (pt + th)))

    level_row = lax.broadcasted_iota(jnp.int32, (depth, cols), 0).astype(jnp.float32)

    def row_face(low_t, low_v, high_t, high_v, h_low, h_high):
        wet = (level_row < h_low).astype(jnp.float32) * (level_row < h_high).astype(jnp.float32)
        return wet * (mix_rows[...] * (high_t - low_t) - 0.25 * (low_v + high_v) * (low_t + high_t))

    first, second = pl.ds(0, depth), pl.ds(depth, depth)
    face_lat[0] = row_face(
        edge_lat[0, first, :], edge_lat[0, second, :], halo_lat[0, first, :], halo_lat[0, second, :],
        own[pl.ds(4 * rows - 1, 1), :], h_north_row,
    )
    face_lat[1] = row_face(
        halo_lat[1, first, :], halo_lat[1, second, :], edge_lat[1, first, :], edge_lat[1, second, :],
        h_south_row, own[pl.ds(3 * rows, 1), :],
    )

    rim_col = last_col | first_col

    def forward(l, sweep):
        at = pl.ds(pl.multiple_of(l * rows, rows), rows)
        rim = jnp.concatenate(
            [
                pltpu.roll(side_flux, cols - 1 - 2 * l, axis=1),
                pltpu.roll(side_flux, lax.rem(2 * cols - 1 - 2 * (l + depth), cols), axis=1),
            ],
            axis=0,
        )
        gain = jnp.where(rim_col, rim, 0.0) + (
            jnp.where(last_row, face_lat[0, pl.ds(l, 1), :], 0.0)
            - jnp.where(first_row, face_lat[1, pl.ds(l, 1), :], 0.0)
        )
        sweep = ((step_ref[at, :] + gain) + cpl[at, :] * sweep) * rec[at, :]
        step_ref[at, :] = sweep
        return sweep

    lax.fori_loop(0, depth, forward, zero, unroll=4)

    def backward(i, x):
        l = depth - 1 - i
        at = pl.ds(pl.multiple_of(l * rows, rows), rows)
        x = step_ref[at, :] - prime[at, :] * x
        tracer_out[at, :] = x
        return x

    lax.fori_loop(0, depth, backward, zero, unroll=4)

    for role, size, target in members:

        @pl.when(role & jnp.logical_not(keeper))
        def _(size=size, target=target):
            ring_hello()
            chain_wait(0, size)
            chain_wait(1, size)

            @pl.when(has_next)
            def _():
                chain_copy(1, size).start()

            first_slot = lowest(me, at_group)
            turned = jnp.where(rising, 1, 0)

            def either(e):
                which = ((wanted(me, group + e) >> 2) - first_slot + turned) & 1
                return jnp.where(
                    jnp.full((size, cols), which, jnp.int32) == 1,
                    fwd_in[1, pl.ds(0, size), :],
                    fwd_in[0, pl.ds(0, size), :],
                )

            serve(size, either, target)

            def hand_on(slot, carry):
                chain_wait(slot, size)
                chain_copy(slot, size).start()
                return carry

            lax.fori_loop(2, blocks, hand_on, 0)

    def source_of(shape, shift, isu):
        s = lax.broadcasted_iota(jnp.int32, shape, 1)
        l = (jnp.full(shape, r, jnp.int32) - isu - s) & (cols - 1)
        return s, l

    @pl.when(top)
    def _():
        shape = (block, cols)
        row = lax.broadcasted_iota(jnp.int32, shape, 0)
        isu = (((row >= 8) & (row < 16)) | ((row >= 24 + SUB) & (row < 16 + 2 * SUB))).astype(jnp.int32)
        s, l = source_of(shape, 0, isu)
        whole = n_lon * cols
        base = jnp.full(shape, pivot_col - lon * cols + 2 * whole, jnp.int32) - isu
        dev_main = ((base - l) & (whole - 1)) >> 7
        off = jnp.where(l < cols // 2, cols, -cols)
        dev_side = ((base - l - off) & (whole - 1)) >> 7
        main = jnp.zeros(shape, jnp.float32)
        side = main
        for e in range(GROUP):
            @pl.when(e != me)
            def _():
                trac_wait(fin.at[e], fin_recv.at[e])

            @pl.when(e == me)
            def _():
                fin[e] = pick[e]

        for e in range(GROUP):
            got = fin[e]
            src = jnp.full(shape, wanted(kind_of(e), lon), jnp.int32)
            main = jnp.where(dev_main == src, got, main)
            side = jnp.where(dev_side == src, got, side)
        main = jnp.take_along_axis(main, l, axis=1)
        side = jnp.take_along_axis(side, l, axis=1)
        for f in range(4):
            ff = (0, 1, 3, 2)[f]
            rest = 32 + (SUB - 8) * f
            for half_of, part in ((west_half, main), (east_half, side)):
                ext[ff, pl.ds(high, 8), half_of] = part[8 * f : 8 * f + 8]
                ext[ff, pl.ds(high + 8, SUB - 8), half_of] = part[rest : rest + SUB - 8]
        for half_of, part in ((west_half, main), (east_half, side)):
            fold_fix[pl.ds(high - 24, 1), half_of] = part[block - 8 : block - 7] - ext[2, pl.ds(high - 1, 1), half_of]

    wide = 2 * cols
    tall = rows + 2 * SUB
    h = ext[3]
    sea = (h > 0.0).astype(jnp.float32)

    def east(x):
        return pltpu.roll(x, wide - 1, axis=1)

    def north(x):
        return pltpu.roll(x, tall - 1, axis=0)

    zonal_mask = sea * east(sea)
    merid_mask = sea * north(sea)
    coef[0] = fb_step * ((h + east(h)) / (2.0 * depth)) * zonal_mask
    coef[1] = (1.0 - drag_rate) * zonal_mask
    coef[2] = fb_step * ((h + north(h)) / (2.0 * depth)) * merid_mask
    coef[3] = (1.0 - drag_rate) * merid_mask
    coef[4] = fb_step * sea
    coef[5] = pltpu.roll(coef[0], 1, axis=1)
    coef[6] = pltpu.roll(coef[1], 1, axis=1)
    coef[7] = pltpu.roll(coef[2], 1, axis=0)
    coef[8] = pltpu.roll(coef[3], 1, axis=0)

    def west(x):
        return pltpu.roll(x, 1, axis=1)

    def south(x):
        return pltpu.roll(x, 1, axis=0)

    def cycle(i, state):
        eta, u, u_west, v, v_south = state
        eta = eta - coef[4] * ((u - u_west) + (v - v_south))
        u = u * coef[1] - coef[0] * (east(eta) - eta)
        v = v * coef[3] - coef[2] * (north(eta) - eta)
        u_west = u_west * coef[6] - coef[5] * (eta - west(eta))
        v_south = v_south * coef[8] - coef[7] * (eta - south(eta))
        return eta, u, u_west, v, v_south

    v_south = south(ext[2])
    v_south = jnp.concatenate([v_south[:24], v_south[24:32] + fold_fix[...], v_south[32:]], axis=0)
    eta, u, _, v, _ = lax.fori_loop(0, SUB, cycle, (ext[0] * sea, ext[1], west(ext[1]), ext[2], v_south), unroll=4)
    surface_out[...] = eta[low:high, :cols]
    transport_out[pl.ds(0, rows), :] = u[low:high, :cols]
    transport_out[pl.ds(rows, rows), :] = v[low:high, :cols]

    @pl.when(top)
    def _():
        got = []
        for j in range(2):
            shape = (depth, cols)
            s, l = source_of(shape, 0, 0)
            whole = n_lon * cols
            dev = ((jnp.full(shape, pivot_col - lon * cols + 2 * whole, jnp.int32) - l) & (whole - 1)) >> 7
            acc = jnp.zeros(shape, jnp.float32)
            for e in range(GROUP):
                trac_wait(tfin.at[j, e], tfin_recv.at[j, e])
                acc = jnp.where(dev == jnp.full(shape, wanted(kind_of(e), lon), jnp.int32), tfin[j, e], acc)
            got.append(jnp.take_along_axis(acc, l, axis=1))
        h_last = own[pl.ds(4 * rows - 1, 1), :]
        flux = row_face(
            edge_lat[0, first, :], edge_lat[0, second, :], got[0], got[1], h_last, ext[3, pl.ds(high, 1), west_half]
        )
        face_lat[0] = (level_row < h_last).astype(jnp.float32) * flux
        c_last = cpl[pl.ds(rows - 1, depth, stride=rows), :]
        r_last = rec[pl.ds(rows - 1, depth, stride=rows), :]
        p_last = prime[pl.ds(rows - 1, depth, stride=rows), :]
        out_last = tracer_out[pl.ds(rows - 1, depth, stride=rows), :]
        delta = face_lat[0]
        sweeps = []
        x = jnp.zeros((1, cols), jnp.float32)
        for k in range(depth):
            x = (delta[k : k + 1] + c_last[k : k + 1] * x) * r_last[k : k + 1]
            sweeps.append(x)
        x = jnp.zeros((1, cols), jnp.float32)
        for k in range(depth - 1, -1, -1):
            x = sweeps[k] - p_last[k : k + 1] * x
            tracer_out[pl.ds(k * rows + rows - 1, 1), :] = out_last[k : k + 1] + x

    for side in (E, W):
        halo_copy(side).wait_send()
    lon_copy(True).wait_send()
    lon_copy(False).wait_send()

    @pl.when(jnp.logical_not(top))
    def _():
        for side in (N, NE, NW):
            halo_copy(side).wait_send()
        lat_copy(True).wait_send()

    @pl.when(jnp.logical_not(bottom))
    def _():
        for side in (S, SE, SW):
            halo_copy(side).wait_send()
        lat_copy(False).wait_send()

    @pl.when(top)
    def _():
        spread_copy(0).wait_send()
        spread_copy(1).wait_send()

        hold_copy(block).wait_send()

        @pl.when(keeper)
        def _():
            for j in range(rise):
                forward_copy(j, j, partner(1), block).wait_send()
            for j in range(fall):
                forward_copy(rise + j, j, partner(n_group - 1), block).wait_send()

        @pl.when(has_next)
        def _():
            def gone(slot, carry):
                chain_copy(slot, block).wait_send()
                return carry

            lax.fori_loop(1, blocks, gone, 0)

        for e in range(GROUP):

            @pl.when(e != me)
            def _(e=e):
                final_copy(e, block, fin.at[me], fin_recv.at[me]).wait_send()

    @pl.when(relay)
    def _():
        hold_copy(depth).wait_send()

        @pl.when(keeper)
        def _():
            for j in range(rise):
                forward_copy(j, j, partner(1), depth).wait_send()
            for j in range(fall):
                forward_copy(rise + j, j, partner(n_group - 1), depth).wait_send()

        @pl.when(has_next)
        def _():
            def gone(slot, carry):
                chain_copy(slot, depth).wait_send()
                return carry

            lax.fori_loop(1, blocks, gone, 0)

        for e in range(GROUP):
            final_copy(e, depth, tfin.at[0, me], tfin_recv.at[0, me]).wait_send()


def write_out(a, b, c, a_hbm, b_hbm, c_hbm, sem):
    copies = [
        pltpu.make_async_copy(src, dst, sem.at[i])
        for i, (src, dst) in enumerate(((a, a_hbm), (b, b_hbm), (c, c_hbm)))
    ]
    for copy in copies:
        copy.start()
    for copy in copies:
        copy.wait()


def solution(mesh):
    n_lon, n_lat = mesh.shape["lon"], mesh.shape["lat"]

    def shards(tracer, velocity, surface, transport, horiz_mixing, vert_mixing, levels, land_tiles, fold_pair):
        depth, rows, cols = tracer.shape
        f32 = jnp.float32
        hbm = pl.BlockSpec(memory_space=pl.ANY)
        vmem = pl.BlockSpec(memory_space=pltpu.VMEM)
        dma = pltpu.SemaphoreType.DMA
        field = pltpu.VMEM((depth * rows, cols), f32)
        results = pl.pallas_call(
            functools.partial(ocean_kernel, n_lon, n_lat, depth, rows, cols),
            name="ocean",
            out_shape=(
                pltpu.VMEM((depth * rows, cols), f32),
                pltpu.VMEM((rows, cols), f32),
                pltpu.VMEM((2 * rows, cols), f32),
            ),
            in_specs=[hbm] * 9,
            out_specs=(vmem, vmem, vmem),
            scratch_shapes=[
                pltpu.SMEM((depth,), f32),
                pltpu.SMEM((depth - 1,), f32),
                pltpu.SMEM((1, 1), jnp.int32),
                pltpu.SMEM((cols,), jnp.int32),
                field,
                pltpu.VMEM((2 * depth * rows, cols), f32),
                pltpu.VMEM((rows, cols), jnp.int32),
                pltpu.VMEM((4 * rows, cols), f32),
                pltpu.VMEM((2, 4 * rows, cols), f32),
                pltpu.VMEM((2, 8, cols), f32),
                pltpu.VMEM((8, 8, cols), f32),
                pltpu.VMEM((16, cols), f32),
                pltpu.VMEM((2, 16, cols), f32),
                pltpu.VMEM((2, 2 * depth, cols), f32),
                pltpu.VMEM((2, 2 * depth, cols), f32),
                pltpu.VMEM((4 * SUB + 8, cols), f32),
                pltpu.VMEM((n_lon // GROUP, 4 * SUB + 8, cols), f32),
                pltpu.VMEM((n_lon // GROUP + 1, 4 * SUB + 8, cols), f32),
                pltpu.VMEM((n_lon // GROUP // 2 + 1, 4 * SUB + 8, cols), f32),
                pltpu.VMEM((GROUP, 4 * SUB + 8, cols), f32),
                pltpu.VMEM((GROUP, 4 * SUB + 8, cols), f32),
                pltpu.VMEM((2, GROUP, depth, cols), f32),
                field,
                field,
                field,
                field,
                pltpu.VMEM((2, depth, cols), f32),
                pltpu.VMEM((depth, cols), f32),
                pltpu.VMEM((4, rows + 2 * SUB, 2 * cols), f32),
                pltpu.VMEM((9, rows + 2 * SUB, 2 * cols), f32),
                pltpu.VMEM((8, 2 * cols), f32),
                dma((9,)),
                pltpu.SemaphoreType.REGULAR((2,)),
                dma((8,)),
                dma((8,)),
                dma((6,)),
                dma((5,)),
                dma((1,)),
                dma((n_lon // GROUP,)),
                dma((n_lon // GROUP + 1,)),
                dma((n_lon // GROUP // 2 + 1,)),
                dma((GROUP,)),
                dma((GROUP,)),
                dma((2, GROUP)),
            ],
            compiler_params=pltpu.CompilerParams(collective_id=1, has_side_effects=True),
        )(
            tracer.reshape(depth * rows, cols),
            velocity.reshape(2 * depth * rows, cols),
            surface,
            transport.reshape(2 * rows, cols),
            levels,
            horiz_mixing,
            vert_mixing,
            land_tiles,
            fold_pair,
        )
        results = [pltpu.with_memory_space_constraint(result, pltpu.VMEM) for result in results]
        tracer_new, surface_new, transport_new = pl.pallas_call(
            write_out,
            name="write_out",
            out_shape=tuple(jax.ShapeDtypeStruct(result.shape, f32) for result in results),
            in_specs=[vmem] * 3,
            out_specs=(hbm,) * 3,
            scratch_shapes=[dma((3,))],
        )(*results)
        return (
            tracer_new.reshape(depth, rows, cols),
            surface_new,
            transport_new.reshape(2, rows, cols),
        )

    return jax.shard_map(
        shards,
        mesh=mesh,
        in_specs=(
            P("member", "lat", "lon"),
            P(None, "member", "lat", "lon"),
            P(("member", "lat"), "lon"),
            P("member", "lat", "lon"),
            P("member"),
            P("member"),
            P("lat", "lon"),
            P("lat", "lon"),
            P("lon"),
        ),
        out_specs=(
            P("member", "lat", "lon"),
            P(("member", "lat"), "lon"),
            P("member", "lat", "lon"),
        ),
        check_vma=False,
    )
```
